1024 devices in a mesh: ctx: 256 (over z, y, core), head: 4 (over x).
Axes of the slice: x: 4, y: 4, z: 32, core: 2. Of those that a mesh axis runs over, the one named last changes fastest.
Arguments:
- queries: bfloat16 [65536, 4096], P('ctx', 'head'), parts along dimension 1, may hold values from -4.6 to 4.6
- key_vectors: bfloat16 [65536, 512], P('ctx', 'head'), parts along dimension 1, may hold values from -4.6 to 4.6
- value_vectors: bfloat16 [65536, 512], P('ctx', 'head'), parts along dimension 1, may hold values from -6 to 6
- doc_ids: int32 [65536], replicated, may hold values from 0 to 169, never falling along the last dimension, each value on 1 to 768 neighbouring positions
- grad_out: bfloat16 [65536, 4096], P('ctx', 'head'), parts along dimension 1, may hold values from -6 to 6
Outputs:
- attended: bfloat16 [65536, 4096], P('ctx', 'head'), parts along dimension 1
- grad_query: bfloat16 [65536, 4096], P('ctx', 'head'), parts along dimension 1
- grad_key: bfloat16 [65536, 512], P('ctx', 'head'), parts along dimension 1
- grad_value: bfloat16 [65536, 512], P('ctx', 'head'), parts along dimension 1
The draws below stay inside these ranges and needn't reach their ends.
There are 4 independent parts, one for each index of `head`. The reference program is written for one: setup_inputs(seed, part) draws one part's arguments, and reference() takes and returns one part's arrays. A program takes and returns all parts, laid end to end along the dimension named above; an argument that names none is the same for every part. Nothing has to cross between parts.
Inputs may be any that keep to these rules, and one draw needn't show every extreme that they name: doc_ids never fall along the sequence; each document holds 1 to 768 positions and one holds exactly 768.
All inputs are finite; a program needn't handle non-finite values.
Results may differ from the reference program's by a relative error of at most 0.029.
Values may be sent and summed in bfloat16 or wider, within the bound.
A program may use at most 32 MiB of HBM per device.

```python
import math
import jax
import jax.numpy as jnp
import numpy as np
from jax import lax

HD = 128
QH = 8
TOK_DEV = 256
REACH = 3
TOKENS = 65536
MOST = 768
DOCS = 170
N_CTX = 256


def draw_key_vectors(key, part):
    drawn = jnp.clip(jax.random.normal(jax.random.fold_in(key, 1), (TOKENS, HD), jnp.float32), -4.6, 4.6)
    return drawn.astype(jnp.bfloat16)


def draw_queries(key, part):
    drawn = jnp.clip(jax.random.normal(jax.random.fold_in(key, 2), (TOKENS, QH * HD), jnp.float32), -4.6, 4.6)
    return drawn.astype(jnp.bfloat16)


def level_of(stream_key, extent, cuts, smallest, high):
    def one(axis_at, parts):
        draws = jax.random.uniform(jax.random.fold_in(jax.random.fold_in(stream_key, 6), axis_at), (parts,), jnp.float32, smallest / len(cuts), high / len(cuts))
        return jnp.repeat(jnp.exp(draws), extent[axis_at] // parts).reshape((-1,) + (1,) * (len(extent) - axis_at - 1))

    loudness = one(*cuts[0])
    for cut in cuts[1:]:
        loudness = loudness * one(*cut)
    return loudness


def profile(count, total, most, slope):
    loads = [(1 << 20) // math.isqrt(grade ** slope) + 1 for grade in range(2, count + 1)]
    spare, counts = total - most - (count - 1), [1] * (count - 1)
    while spare > 0:
        candidates = [i for i in range(count - 1) if counts[i] < most]
        mass, left = sum([loads[i] for i in candidates]), spare
        for i in candidates:
            extra = min(most - counts[i], max(1, left * loads[i] // mass), spare)
            counts[i] = counts[i] + extra
            spare = spare - extra
    return np.array([most] + counts)


def uneven_parts(own_key, count, total, most, slope):
    if count == 2:
        one = jax.random.randint(own_key, (), max(1, total - most), min(most, total - 1) + 1)
        return jnp.stack([one, total - one])
    lengths = jnp.asarray(profile(count, total, most, slope), jnp.int32)
    couples = (count - 1) // 2
    giver, taker = lengths[1:1 + 2 * couples:2], lengths[2:2 + 2 * couples:2]
    margin = jnp.minimum(giver - 1, most - taker)
    shifted = jax.random.randint(jax.random.fold_in(own_key, 1), (couples,), 0, 1 << 20) % (margin + 1)
    lengths = lengths.at[1:1 + 2 * couples:2].set(giver - shifted).at[2:2 + 2 * couples:2].set(taker + shifted)
    return lengths[jax.random.permutation(jax.random.fold_in(own_key, 2), count)]


def noise(own_key, extent, scale, most, cuts=(), kind=jnp.bfloat16):
    array = scale * jax.random.normal(own_key, extent, jnp.float32)
    if cuts:
        array = array * level_of(own_key, extent, cuts, -0.22, 0.18)
    return jnp.clip(array, -most, most).astype(kind)


def setup_inputs(seed: int = 0, part: int = 0) -> dict:
    key_list = jax.random.split(jax.random.key(seed), 6)
    part_splits = jax.random.split(jax.random.fold_in(key_list[5], part), 6)
    return {
        "queries": draw_queries(jax.random.fold_in(jax.random.fold_in(key_list[5], part), 71), part),
        "key_vectors": draw_key_vectors(jax.random.fold_in(jax.random.fold_in(key_list[5], part), 71), part),
        "value_vectors": noise(part_splits[2], (TOKENS, HD), 1.0, 6.0, ((0, 256),)),
        "doc_ids": jnp.searchsorted(jnp.cumsum(uneven_parts(key_list[3], DOCS, TOKENS, MOST, 1)), jnp.arange(TOKENS), side="right").astype(jnp.int32),
        "grad_out": noise(part_splits[4], (TOKENS, QH * HD), 1.0, 6.0, ((0, 256),)),
    }


def block_grads(query_rows, grad_rows, key_value, query_pos, key_pos, query_doc, key_doc):
    row_count = query_rows.shape[0]
    head_dim = key_value.shape[1] // 2
    score_scale = head_dim ** -0.5
    query_heads = query_rows.astype(jnp.float32).reshape(row_count, -1, head_dim)
    grad_heads = grad_rows.astype(jnp.float32).reshape(row_count, -1, head_dim)
    key_part = key_value[:, :head_dim].astype(jnp.float32)
    value_part = key_value[:, head_dim:].astype(jnp.float32)
    allowed = (query_doc[:, None] == key_doc[None, :]) & (key_pos[None, :] <= query_pos[:, None]) & (key_pos[None, :] >= 0)
    scores = jnp.einsum("thd,kd->htk", query_heads, key_part) * score_scale
    scores = jnp.where(allowed[None], scores, -1e30)
    row_max = jnp.max(scores, axis=-1, keepdims=True)
    row_sum = jnp.sum(jnp.where(allowed[None], jnp.exp(scores - row_max), 0.0), axis=-1, keepdims=True)
    log_norm = row_max + jnp.log(row_sum)
    probs = jnp.where(allowed[None], jnp.exp(scores - log_norm), 0.0)
    weights = probs.astype(jnp.bfloat16).astype(jnp.float32)
    attended = jnp.einsum("htk,kd->thd", weights, value_part).astype(jnp.bfloat16)
    delta = jnp.sum(grad_heads * attended.astype(jnp.float32), axis=-1)
    grad_prob = jnp.einsum("thd,kd->htk", grad_heads, value_part)
    dscore = (probs * (grad_prob - jnp.transpose(delta)[:, :, None])).astype(jnp.bfloat16).astype(jnp.float32)
    grad_query = (jnp.einsum("htk,kd->thd", dscore, key_part) * score_scale).astype(jnp.bfloat16)
    grad_key = jnp.einsum("htk,thd->kd", dscore, query_heads) * score_scale
    grad_value = jnp.einsum("htk,thd->kd", weights, grad_heads)
    return attended.reshape(row_count, -1), grad_query.reshape(row_count, -1), jnp.concatenate([grad_key, grad_value], axis=1)


def reference(queries, key_vectors, value_vectors, doc_ids, grad_out):
    row_count = TOK_DEV
    key_span = (REACH + 1) * row_count
    key_value = jnp.concatenate([key_vectors, value_vectors], axis=1)
    padded_kv = jnp.concatenate([jnp.zeros((REACH * row_count, 2 * HD), jnp.bfloat16), key_value], axis=0)
    padded_doc = jnp.concatenate([jnp.full((REACH * row_count,), -1, jnp.int32), doc_ids.astype(jnp.int32)], axis=0)

    def one_block(totals, block_no):
        first_row = (block_no * row_count).astype(jnp.int32)
        query_rows = lax.dynamic_slice_in_dim(queries, first_row, row_count, 0)
        grad_rows = lax.dynamic_slice_in_dim(grad_out, first_row, row_count, 0)
        window = lax.dynamic_slice_in_dim(padded_kv, first_row, key_span, 0)
        key_doc = lax.dynamic_slice_in_dim(padded_doc, first_row, key_span, 0)
        query_doc = lax.dynamic_slice_in_dim(doc_ids.astype(jnp.int32), first_row, row_count, 0)
        query_pos = first_row + jnp.arange(row_count, dtype=jnp.int32)
        key_pos = first_row - REACH * row_count + jnp.arange(key_span, dtype=jnp.int32)
        attended, grad_query, grad_pair = block_grads(query_rows, grad_rows, window, query_pos, key_pos, query_doc, key_doc)
        current = lax.dynamic_slice_in_dim(totals, first_row, key_span, 0)
        totals = lax.dynamic_update_slice_in_dim(totals, current + grad_pair, first_row, 0)
        return totals, (attended, grad_query)

    start_totals = jnp.zeros((REACH * row_count + TOKENS, 2 * HD), jnp.float32)
    totals, (attended, grad_query) = lax.scan(one_block, start_totals, jnp.arange(N_CTX, dtype=jnp.int32))
    grad_pair = totals[REACH * row_count:]
    return (attended.reshape(TOKENS, QH * HD), grad_query.reshape(TOKENS, QH * HD),
            grad_pair[:, :HD].astype(jnp.bfloat16), grad_pair[:, HD:].astype(jnp.bfloat16))
```

```python
import functools
import math

import jax
import jax.numpy as jnp
from jax import lax
from jax.experimental import pallas as pl
from jax.experimental.pallas import tpu as pltpu
from jax.sharding import PartitionSpec as P

REACH = 3
OWN = REACH
F32 = jnp.float32
BF16 = jnp.bfloat16
MESH = pl.DeviceIdType.MESH
NT = (((1,), (1,)), ((), ()))
NN = (((1,), (0,)), ((), ()))


def dot(a, b, dims=NN):
    return lax.dot_general(a, b, dims, preferred_element_type=F32)


def fill_bias(doc, bias):
    rows = doc.shape[2]
    total = doc.shape[1] * rows
    query_doc = jnp.concatenate([doc[OWN, i : i + 1, :] for i in range(doc.shape[1])], axis=1)
    query_doc = jnp.broadcast_to(query_doc, (rows, total))
    for part in range(doc.shape[1]):

        def column(slot):
            line = jnp.broadcast_to(doc[slot, part : part + 1, :], (rows, rows))
            return jnp.broadcast_to(jnp.transpose(line)[:, 0:1], (rows, total))

        key_at = lax.broadcasted_iota(jnp.int32, (rows, total), 0) + part * rows
        query_at = lax.broadcasted_iota(jnp.int32, (rows, total), 1)
        folded = jnp.where(key_at <= query_at, column(OWN), column(0))
        for block, key_doc in ((0, folded), (1, column(1)), (2, column(2))):
            bias[block, pl.ds(part * rows, rows), :] = jnp.where(key_doc == query_doc, 0.0, -1e30)


def kernel(
    n,
    q_hbm,
    g_hbm,
    k_hbm,
    v_hbm,
    doc_hbm,
    att_ref,
    dq_ref,
    dk_ref,
    dv_ref,
    q,
    g,
    keys,
    values,
    doc,
    bias,
    weights,
    dscores,
    own_grad,
    out_grad,
    in_grad,
    local_sem,
    kv_send,
    kv_recv,
    grad_send,
    grad_recv,
):
    heads, rows, dim = q.shape
    scale = 1.0 / math.sqrt(dim)
    me = lax.axis_index("ctx")

    local = []
    for slot in range(REACH + 1):
        block = lax.rem(me + n - REACH + slot, n)
        local.append(pltpu.make_async_copy(doc_hbm.at[block], doc.at[slot], local_sem.at[0, slot]))
    local.append(pltpu.make_async_copy(k_hbm, keys.at[OWN], local_sem.at[0, 4]))
    local.append(pltpu.make_async_copy(v_hbm, values.at[OWN], local_sem.at[0, 5]))
    for h in range(heads):
        columns = pl.ds(h * dim, dim)
        local.append(pltpu.make_async_copy(q_hbm.at[:, columns], q.at[h], local_sem.at[1, h]))
        local.append(pltpu.make_async_copy(g_hbm.at[:, columns], g.at[h], local_sem.at[2, h]))
    for copy in local:
        copy.start()

    barrier = pltpu.get_barrier_semaphore()
    for d in range(1, REACH + 1):
        for other in (lax.rem(me + d, n), lax.rem(me + n - d, n)):
            pl.semaphore_signal(barrier, inc=1, device_id={"ctx": other}, device_id_type=MESH)
    pl.semaphore_wait(barrier, 2 * REACH)

    moves = []
    for which, (source, target) in enumerate(((k_hbm, keys), (v_hbm, values))):
        for d in range(1, REACH + 1):
            moves.append(
                pltpu.make_async_remote_copy(
                    src_ref=source,
                    dst_ref=target.at[REACH - d],
                    send_sem=kv_send.at[which, d - 1],
                    recv_sem=kv_recv.at[which, d - 1],
                    device_id={"ctx": lax.rem(me + d, n)},
                    device_id_type=MESH,
                )
            )
    for move in moves:
        move.start()

    for copy in local[: REACH + 1]:
        copy.wait()
    fill_bias(doc, bias)
    for copy in local[REACH + 1 :]:
        copy.wait()
    for move in moves:
        move.wait()

    exponent = math.log2(math.e) * scale
    key_at = lax.broadcasted_iota(jnp.int32, (rows, rows), 0)
    query_at = lax.broadcasted_iota(jnp.int32, (rows, rows), 1)
    own = key_at <= query_at
    for h in range(heads):
        columns = pl.ds(h * rows, rows)
        s = [dot(keys[j], q[h], NT) for j in range(REACH + 1)]
        s = [jnp.where(own, s[OWN], s[0]) + bias[0], s[1] + bias[1], s[2] + bias[2]]
        top = jnp.maximum(jnp.maximum(s[0], s[1]), s[2]).max(axis=0, keepdims=True)
        e = [jnp.exp2((x - top) * exponent) for x in s]
        inverse = 1.0 / (e[0] + e[1] + e[2]).sum(axis=0, keepdims=True)
        d = [dot(values[j], g[h], NT) for j in range(REACH + 1)]
        d = [jnp.where(own, d[OWN], d[0]), d[1], d[2]]
        w = [x * inverse for x in e]
        delta = (w[0] * d[0] + w[1] * d[1] + w[2] * d[2]).sum(axis=0, keepdims=True)
        ds = [x * (y - delta) for x, y in zip(w, d)]
        for ref, v in ((weights, w), (dscores, ds)):
            ref[0, :, columns] = jnp.where(own, 0.0, v[0]).astype(BF16)
            ref[OWN, :, columns] = jnp.where(own, v[0], 0.0).astype(BF16)
            ref[1, :, columns] = v[1].astype(BF16)
            ref[2, :, columns] = v[2].astype(BF16)

    sends = []
    for j in range(REACH + 1):
        dv = dot(weights[j], g[...].reshape(heads * rows, dim))
        dk = dot(dscores[j], q[...].reshape(heads * rows, dim)) * scale
        if j == OWN:
            own_grad[0] = dk
            own_grad[1] = dv
            continue
        d = REACH - j
        out_grad[d - 1, 0] = dk.astype(BF16)
        out_grad[d - 1, 1] = dv.astype(BF16)
        sends.append(
            pltpu.make_async_remote_copy(
                src_ref=out_grad.at[d - 1],
                dst_ref=in_grad.at[d - 1],
                send_sem=grad_send.at[d - 1],
                recv_sem=grad_recv.at[d - 1],
                device_id={"ctx": lax.rem(me + n - d, n)},
                device_id_type=MESH,
            )
        )
        sends[-1].start()

    keys_t = [jnp.transpose(keys[j]) for j in range(REACH + 1)]
    values_t = [jnp.transpose(values[j]) for j in range(REACH + 1)]
    for h in range(heads):
        columns = pl.ds(h * rows, rows)
        att = sum(dot(values_t[j], weights[j, :, columns]) for j in range(REACH + 1))
        att_ref[:, pl.ds(h * dim, dim)] = jnp.transpose(att).astype(BF16)
        dq = sum(dot(keys_t[j], dscores[j, :, columns]) for j in range(REACH + 1)) * scale
        dq_ref[:, pl.ds(h * dim, dim)] = jnp.transpose(dq).astype(BF16)

    for send in sends:
        send.wait()
    for which, ref in ((0, dk_ref), (1, dv_ref)):
        total = own_grad[which]
        for d in range(REACH):
            total = total + in_grad[d, which].astype(F32)
        ref[...] = total.astype(BF16)


def hand_over(*refs):
    count = (len(refs) - 1) // 2
    sem = refs[-1]
    copies = [
        pltpu.make_async_copy(refs[i], refs[count + i], sem.at[i]) for i in range(count)
    ]
    for copy in copies:
        copy.start()
    for copy in copies:
        copy.wait()


def body(n, queries, key_vectors, value_vectors, doc_ids, grad_out):
    rows, width = queries.shape
    dim = key_vectors.shape[1]
    heads = width // dim
    lanes = 128
    doc = doc_ids.reshape(n, rows // lanes, lanes)
    hbm = pl.BlockSpec(memory_space=pltpu.HBM)
    vmem = pl.BlockSpec(memory_space=pltpu.VMEM)
    shapes = [
        jax.ShapeDtypeStruct((rows, width), BF16),
        jax.ShapeDtypeStruct((rows, width), BF16),
        jax.ShapeDtypeStruct((rows, dim), BF16),
        jax.ShapeDtypeStruct((rows, dim), BF16),
    ]
    blocks = REACH + 1
    results = pl.pallas_call(
        functools.partial(kernel, n),
        out_shape=shapes,
        in_specs=[hbm] * 5,
        out_specs=[vmem] * 4,
        scratch_shapes=[
            pltpu.VMEM((heads, rows, dim), BF16),
            pltpu.VMEM((heads, rows, dim), BF16),
            pltpu.VMEM((blocks, rows, dim), BF16),
            pltpu.VMEM((blocks, rows, dim), BF16),
            pltpu.VMEM((blocks, rows // lanes, lanes), jnp.int32),
            pltpu.VMEM((REACH, rows, rows), F32),
            pltpu.VMEM((blocks, rows, heads * rows), BF16),
            pltpu.VMEM((blocks, rows, heads * rows), BF16),
            pltpu.VMEM((2, rows, dim), F32),
            pltpu.VMEM((REACH, 2, rows, dim), BF16),
            pltpu.VMEM((REACH, 2, rows, dim), BF16),
            pltpu.SemaphoreType.DMA((3, 8)),
            pltpu.SemaphoreType.DMA((2, REACH)),
            pltpu.SemaphoreType.DMA((2, REACH)),
            pltpu.SemaphoreType.DMA((REACH,)),
            pltpu.SemaphoreType.DMA((REACH,)),
        ],
        compiler_params=pltpu.CompilerParams(
            collective_id=0, has_side_effects=True, vmem_limit_bytes=40 << 20
        ),
    )(queries, grad_out, key_vectors, value_vectors, doc)
    return pl.pallas_call(
        hand_over,
        out_shape=shapes,
        in_specs=[vmem] * 4,
        out_specs=[hbm] * 4,
        scratch_shapes=[pltpu.SemaphoreType.DMA((4,))],
        compiler_params=pltpu.CompilerParams(vmem_limit_bytes=8 << 20),
    )(*results)


def solution(mesh):
    return jax.shard_map(
        functools.partial(body, mesh.shape["ctx"]),
        mesh=mesh,
        in_specs=(P("ctx", "head"), P("ctx", "head"), P("ctx", "head"), P(), P("ctx", "head")),
        out_specs=(P("ctx", "head"), P("ctx", "head"), P("ctx", "head"), P("ctx", "head")),
        check_vma=False,
    )
```

```python
import functools
import math

import jax
import jax.numpy as jnp
from jax import lax
from jax.experimental import pallas as pl
from jax.experimental.pallas import tpu as pltpu
from jax.sharding import PartitionSpec as P

REACH = 3
OWN = REACH
F32 = jnp.float32
BF16 = jnp.bfloat16
MESH = pl.DeviceIdType.MESH
NT = (((1,), (1,)), ((), ()))
NN = (((1,), (0,)), ((), ()))


def dot(a, b, dims=NN):
    return lax.dot_general(a, b, dims, preferred_element_type=F32)


def fill_bias(doc, bias):
    rows = doc.shape[2]
    total = doc.shape[1] * rows
    query_doc = jnp.concatenate([doc[OWN, i : i + 1, :] for i in range(doc.shape[1])], axis=1)
    query_doc = jnp.broadcast_to(query_doc, (rows, total))
    for part in range(doc.shape[1]):
        for slot in range(REACH + 1):
            line = jnp.broadcast_to(doc[slot, part : part + 1, :], (rows, rows))
            allowed = jnp.broadcast_to(jnp.transpose(line)[:, 0:1], (rows, total)) == query_doc
            if slot == OWN:
                key_at = lax.broadcasted_iota(jnp.int32, (rows, total), 0) + part * rows
                query_at = lax.broadcasted_iota(jnp.int32, (rows, total), 1)
                allowed = allowed & (key_at <= query_at)
            bias[slot, pl.ds(part * rows, rows), :] = jnp.where(allowed, 0.0, -1e30)


def kernel(
    n,
    q_hbm,
    g_hbm,
    k_hbm,
    v_hbm,
    doc_hbm,
    att_ref,
    dq_ref,
    dk_ref,
    dv_ref,
    q,
    g,
    keys,
    values,
    doc,
    bias,
    stats,
    factors,
    raw,
    slopes,
    weights,
    dscores,
    own_grad,
    out_grad,
    in_grad,
    local_sem,
    kv_send,
    kv_recv,
    grad_send,
    grad_recv,
):
    heads, rows, dim = q.shape
    scale = 1.0 / math.sqrt(dim)
    exponent = math.log2(math.e) * scale
    me = lax.axis_index("ctx")
    reach = range(1, REACH + 1)

    local = []
    for slot in range(REACH + 1):
        block = lax.rem(me + n - REACH + slot, n)
        local.append(pltpu.make_async_copy(doc_hbm.at[block], doc.at[slot], local_sem.at[0, slot]))
    local.append(pltpu.make_async_copy(k_hbm, keys.at[OWN], local_sem.at[0, 4]))
    local.append(pltpu.make_async_copy(v_hbm, values.at[OWN], local_sem.at[0, 5]))
    for h in range(heads):
        columns = pl.ds(h * dim, dim)
        local.append(pltpu.make_async_copy(q_hbm.at[:, columns], q.at[h], local_sem.at[1, h]))
        local.append(pltpu.make_async_copy(g_hbm.at[:, columns], g.at[h], local_sem.at[2, h]))
    for copy in local:
        copy.start()

    barrier = pltpu.get_barrier_semaphore()

    def greet(there, other):
        @pl.when(there)
        def _():
            pl.semaphore_signal(barrier, inc=1, device_id={"ctx": other}, device_id_type=MESH)

    for d in reach:

        @pl.when(me < d)
        def _():
            keys[REACH - d] = jnp.zeros(keys.shape[1:], BF16)
            values[REACH - d] = jnp.zeros(values.shape[1:], BF16)

    for d in reach:
        greet(me + d < n, me + d)
        greet(me >= d, me - d)
    for missing in range(REACH + 1):
        if missing:
            here = (me == REACH - missing) | (me == n - 1 - REACH + missing)
        else:
            here = (me >= REACH) & (me < n - REACH)

        @pl.when(here)
        def _():
            pl.semaphore_wait(barrier, 2 * REACH - missing)

    def kv_moves(d):
        return [
            pltpu.make_async_remote_copy(
                src_ref=source,
                dst_ref=target.at[REACH - d],
                send_sem=kv_send.at[which, d - 1],
                recv_sem=kv_recv.at[which, d - 1],
                device_id={"ctx": me + d},
                device_id_type=MESH,
            )
            for which, (source, target) in enumerate(((k_hbm, keys), (v_hbm, values)))
        ]

    def grad_move(d):
        return pltpu.make_async_remote_copy(
            src_ref=out_grad.at[d - 1],
            dst_ref=in_grad.at[d - 1],
            send_sem=grad_send.at[d - 1],
            recv_sem=grad_recv.at[d - 1],
            device_id={"ctx": me - d},
            device_id_type=MESH,
        )

    for d in reach:

        @pl.when(me + d < n)
        def _():
            for move in kv_moves(d):
                move.start()

    for copy in local[: REACH + 1]:
        copy.wait()
    fill_bias(doc, bias)
    stats[0] = jnp.full(stats.shape[1:], -1e30, F32)
    stats[1] = jnp.zeros(stats.shape[1:], F32)
    stats[2] = jnp.zeros(stats.shape[1:], F32)
    for copy in local[REACH + 1 :]:
        copy.wait()

    def first_pass(j):
        for h in range(heads):
            columns = pl.ds(h * rows, rows)
            s = dot(keys[j], q[h], NT) + bias[j]
            top = s.max(axis=0, keepdims=True)
            e = jnp.exp2((s - top) * exponent)
            slope = dot(values[j], g[h], NT)
            stats[0, j, h : h + 1, :] = top
            stats[1, j, h : h + 1, :] = e.sum(axis=0, keepdims=True)
            stats[2, j, h : h + 1, :] = (e * slope).sum(axis=0, keepdims=True)
            raw[j, :, columns] = e
            slopes[j, :, columns] = slope

    first_pass(OWN)
    for d in reach:

        @pl.when(me >= d)
        def _():
            for move in kv_moves(d):
                move.wait_recv()
            first_pass(REACH - d)

    tops = [stats[0, j] for j in range(REACH + 1)]
    top = jnp.maximum(jnp.maximum(tops[0], tops[1]), jnp.maximum(tops[2], tops[3]))
    grown = [jnp.exp2((x - top) * exponent) for x in tops]
    inverse = 1.0 / sum(x * stats[1, j] for j, x in enumerate(grown))
    delta = sum(x * stats[2, j] for j, x in enumerate(grown)) * inverse
    for j in range(REACH + 1):
        factors[j] = grown[j] * inverse
    factors[REACH + 1] = delta

    def second_pass(j):
        for h in range(heads):
            columns = pl.ds(h * rows, rows)
            w = raw[j, :, columns] * factors[j, h : h + 1, :]
            weights[j, :, columns] = w.astype(BF16)
            ds = w * (slopes[j, :, columns] - factors[REACH + 1, h : h + 1, :])
            dscores[j, :, columns] = ds.astype(BF16)
        dv = dot(weights[j], g[...].reshape(heads * rows, dim))
        dk = dot(dscores[j], q[...].reshape(heads * rows, dim)) * scale
        return dk, dv

    for d in reach:
        j = REACH - d

        @pl.when(me >= d)
        def _():
            dk, dv = second_pass(j)
            out_grad[d - 1, 0] = dk.astype(BF16)
            out_grad[d - 1, 1] = dv.astype(BF16)
            grad_move(d).start()

        @pl.when(me < d)
        def _():
            weights[j] = jnp.zeros(weights.shape[1:], BF16)
            dscores[j] = jnp.zeros(dscores.shape[1:], BF16)

    dk, dv = second_pass(OWN)
    own_grad[0] = dk
    own_grad[1] = dv

    keys_t = [jnp.transpose(keys[j]) for j in range(REACH + 1)]
    values_t = [jnp.transpose(values[j]) for j in range(REACH + 1)]
    for h in range(heads):
        columns = pl.ds(h * rows, rows)
        att = sum(dot(values_t[j], weights[j, :, columns]) for j in range(REACH + 1))
        att_ref[:, pl.ds(h * dim, dim)] = jnp.transpose(att).astype(BF16)
        dq = sum(dot(keys_t[j], dscores[j, :, columns]) for j in range(REACH + 1)) * scale
        dq_ref[:, pl.ds(h * dim, dim)] = jnp.transpose(dq).astype(BF16)

    for d in reach:

        @pl.when(me + d < n)
        def _():
            for move in kv_moves(d):
                move.wait_send()
            grad_move(d).wait_recv()
            for which in range(2):
                own_grad[which] += in_grad[d - 1, which].astype(F32)

        @pl.when(me >= d)
        def _():
            grad_move(d).wait_send()

    dk_ref[...] = own_grad[0].astype(BF16)
    dv_ref[...] = own_grad[1].astype(BF16)


def hand_over(*refs):
    count = (len(refs) - 1) // 2
    sem = refs[-1]
    copies = [
        pltpu.make_async_copy(refs[i], refs[count + i], sem.at[i]) for i in range(count)
    ]
    for copy in copies:
        copy.start()
    for copy in copies:
        copy.wait()


def body(n, queries, key_vectors, value_vectors, doc_ids, grad_out):
    rows, width = queries.shape
    dim = key_vectors.shape[1]
    heads = width // dim
    lanes = 128
    doc = doc_ids.reshape(n, rows // lanes, lanes)
    hbm = pl.BlockSpec(memory_space=pltpu.HBM)
    vmem = pl.BlockSpec(memory_space=pltpu.VMEM)
    shapes = [
        jax.ShapeDtypeStruct((rows, width), BF16),
        jax.ShapeDtypeStruct((rows, width), BF16),
        jax.ShapeDtypeStruct((rows, dim), BF16),
        jax.ShapeDtypeStruct((rows, dim), BF16),
    ]
    blocks = REACH + 1
    results = pl.pallas_call(
        functools.partial(kernel, n),
        out_shape=shapes,
        in_specs=[hbm] * 5,
        out_specs=[vmem] * 4,
        scratch_shapes=[
            pltpu.VMEM((heads, rows, dim), BF16),
            pltpu.VMEM((heads, rows, dim), BF16),
            pltpu.VMEM((blocks, rows, dim), BF16),
            pltpu.VMEM((blocks, rows, dim), BF16),
            pltpu.VMEM((blocks, rows // lanes, lanes), jnp.int32),
            pltpu.VMEM((blocks, rows, rows), F32),
            pltpu.VMEM((3, blocks, heads, rows), F32),
            pltpu.VMEM((blocks + 1, heads, rows), F32),
            pltpu.VMEM((blocks, rows, heads * rows), F32),
            pltpu.VMEM((blocks, rows, heads * rows), F32),
            pltpu.VMEM((blocks, rows, heads * rows), BF16),
            pltpu.VMEM((blocks, rows, heads * rows), BF16),
            pltpu.VMEM((2, rows, dim), F32),
            pltpu.VMEM((REACH, 2, rows, dim), BF16),
            pltpu.VMEM((REACH, 2, rows, dim), BF16),
            pltpu.SemaphoreType.DMA((3, 8)),
            pltpu.SemaphoreType.DMA((2, REACH)),
            pltpu.SemaphoreType.DMA((2, REACH)),
            pltpu.SemaphoreType.DMA((REACH,)),
            pltpu.SemaphoreType.DMA((REACH,)),
        ],
        compiler_params=pltpu.CompilerParams(
            collective_id=0, has_side_effects=True, vmem_limit_bytes=48 << 20
        ),
    )(*(pltpu.with_memory_space_constraint(x, pltpu.HBM) for x in (queries, grad_out, key_vectors, value_vectors, doc)))
    return pl.pallas_call(
        hand_over,
        out_shape=shapes,
        in_specs=[vmem] * 4,
        out_specs=[hbm] * 4,
        scratch_shapes=[pltpu.SemaphoreType.DMA((4,))],
        compiler_params=pltpu.CompilerParams(vmem_limit_bytes=8 << 20),
    )(*results)


def solution(mesh):
    return jax.shard_map(
        functools.partial(body, mesh.shape["ctx"]),
        mesh=mesh,
        in_specs=(P("ctx", "head"), P("ctx", "head"), P("ctx", "head"), P(), P("ctx", "head")),
        out_specs=(P("ctx", "head"), P("ctx", "head"), P("ctx", "head"), P("ctx", "head")),
        check_vma=False,
    )
```

```python
import functools
import math

import jax
import jax.numpy as jnp
from jax import lax
from jax.experimental import pallas as pl
from jax.experimental.pallas import tpu as pltpu
from jax.sharding import PartitionSpec as P

REACH = 3
OWN = REACH
F32 = jnp.float32
BF16 = jnp.bfloat16
MESH = pl.DeviceIdType.MESH
NT = (((1,), (1,)), ((), ()))
NN = (((1,), (0,)), ((), ()))


def dot(a, b, dims=NN):
    return lax.dot_general(a, b, dims, preferred_element_type=F32)


def fill_bias(doc, bias):
    rows = doc.shape[2]
    total = doc.shape[1] * rows
    query_doc = jnp.concatenate([doc[OWN, i : i + 1, :] for i in range(doc.shape[1])], axis=1)
    query_doc = jnp.broadcast_to(query_doc, (rows, total))
    for part in range(doc.shape[1]):
        for slot in range(REACH + 1):
            line = jnp.broadcast_to(doc[slot, part : part + 1, :], (rows, rows))
            allowed = jnp.broadcast_to(jnp.transpose(line)[:, 0:1], (rows, total)) == query_doc
            if slot == OWN:
                key_at = lax.broadcasted_iota(jnp.int32, (rows, total), 0) + part * rows
                query_at = lax.broadcasted_iota(jnp.int32, (rows, total), 1)
                allowed = allowed & (key_at <= query_at)
            bias[slot, pl.ds(part * rows, rows), :] = jnp.where(allowed, 0.0, -1e30)


def kernel(
    n,
    q_hbm,
    g_hbm,
    k_hbm,
    v_hbm,
    doc_hbm,
    att_ref,
    dq_ref,
    dk_ref,
    dv_ref,
    q,
    g,
    keys,
    values,
    doc,
    bias,
    stats,
    factors,
    raw,
    slopes,
    weights,
    dscores,
    own_grad,
    out_grad,
    in_grad,
    local_sem,
    kv_send,
    kv_recv,
    grad_send,
    grad_recv,
):
    heads, rows, dim = q.shape
    scale = 1.0 / math.sqrt(dim)
    exponent = math.log2(math.e) * scale
    me = lax.axis_index("ctx")
    reach = range(1, REACH + 1)

    local = []
    for slot in range(REACH + 1):
        block = lax.rem(me + n - REACH + slot, n)
        local.append(pltpu.make_async_copy(doc_hbm.at[block], doc.at[slot], local_sem.at[0, slot]))
    local.append(pltpu.make_async_copy(k_hbm, keys.at[OWN], local_sem.at[0, 4]))
    local.append(pltpu.make_async_copy(v_hbm, values.at[OWN], local_sem.at[0, 5]))
    for h in range(heads):
        columns = pl.ds(h * dim, dim)
        local.append(pltpu.make_async_copy(q_hbm.at[:, columns], q.at[h], local_sem.at[1, h]))
        local.append(pltpu.make_async_copy(g_hbm.at[:, columns], g.at[h], local_sem.at[2, h]))
    for copy in local:
        copy.start()

    barrier = pltpu.get_barrier_semaphore()

    def greet(there, other):
        @pl.when(there)
        def _():
            pl.semaphore_signal(barrier, inc=1, device_id={"ctx": other}, device_id_type=MESH)

    for d in reach:

        @pl.when(me < d)
        def _():
            keys[REACH - d] = jnp.zeros(keys.shape[1:], BF16)
            values[REACH - d] = jnp.zeros(values.shape[1:], BF16)

    for d in reach:
        greet(me >= d, me - d)
    for missing in range(REACH):
        here = me == n - 1 - REACH + missing if missing else me < n - REACH

        @pl.when(here)
        def _():
            pl.semaphore_wait(barrier, REACH - missing)

    def kv_moves(d):
        return [
            pltpu.make_async_remote_copy(
                src_ref=source,
                dst_ref=target.at[REACH - d],
                send_sem=kv_send.at[which, d - 1],
                recv_sem=kv_recv.at[which, d - 1],
                device_id={"ctx": me + d},
                device_id_type=MESH,
            )
            for which, (source, target) in enumerate(((k_hbm, keys), (v_hbm, values)))
        ]

    def grad_move(d):
        return pltpu.make_async_remote_copy(
            src_ref=out_grad.at[d - 1],
            dst_ref=in_grad.at[d - 1],
            send_sem=grad_send.at[d - 1],
            recv_sem=grad_recv.at[d - 1],
            device_id={"ctx": me - d},
            device_id_type=MESH,
        )

    for d in reach:

        @pl.when(me + d < n)
        def _():
            for move in kv_moves(d):
                move.start()

    for copy in local[: REACH + 1]:
        copy.wait()
    fill_bias(doc, bias)
    stats[0] = jnp.full(stats.shape[1:], -1e30, F32)
    stats[1] = jnp.zeros(stats.shape[1:], F32)
    stats[2] = jnp.zeros(stats.shape[1:], F32)
    for copy in local[REACH + 1 :]:
        copy.wait()

    def first_pass(j):
        for h in range(heads):
            columns = pl.ds(h * rows, rows)
            s = dot(keys[j], q[h], NT) + bias[j]
            top = s.max(axis=0, keepdims=True)
            e = jnp.exp2((s - top) * exponent)
            slope = dot(values[j], g[h], NT)
            stats[0, j, h : h + 1, :] = top
            stats[1, j, h : h + 1, :] = e.sum(axis=0, keepdims=True)
            stats[2, j, h : h + 1, :] = (e * slope).sum(axis=0, keepdims=True)
            raw[j, :, columns] = e
            slopes[j, :, columns] = slope

    first_pass(OWN)
    for d in reach:

        @pl.when(me >= d)
        def _():
            for move in kv_moves(d):
                move.wait_recv()
            first_pass(REACH - d)

    tops = [stats[0, j] for j in range(REACH + 1)]
    top = jnp.maximum(jnp.maximum(tops[0], tops[1]), jnp.maximum(tops[2], tops[3]))
    grown = [jnp.exp2((x - top) * exponent) for x in tops]
    inverse = 1.0 / sum(x * stats[1, j] for j, x in enumerate(grown))
    delta = sum(x * stats[2, j] for j, x in enumerate(grown)) * inverse
    for j in range(REACH + 1):
        factors[j] = grown[j] * inverse
    factors[REACH + 1] = delta

    def second_pass(j):
        for h in range(heads):
            columns = pl.ds(h * rows, rows)
            w = raw[j, :, columns] * factors[j, h : h + 1, :]
            weights[j, :, columns] = w.astype(BF16)
            ds = w * (slopes[j, :, columns] - factors[REACH + 1, h : h + 1, :])
            dscores[j, :, columns] = ds.astype(BF16)
        dv = dot(weights[j], g[...].reshape(heads * rows, dim))
        dk = dot(dscores[j], q[...].reshape(heads * rows, dim)) * scale
        return dk, dv

    for d in reach:
        j = REACH - d

        @pl.when(me >= d)
        def _():
            dk, dv = second_pass(j)
            out_grad[d - 1, 0] = dk.astype(BF16)
            out_grad[d - 1, 1] = dv.astype(BF16)
            grad_move(d).start()

        @pl.when(me < d)
        def _():
            weights[j] = jnp.zeros(weights.shape[1:], BF16)
            dscores[j] = jnp.zeros(dscores.shape[1:], BF16)

    dk, dv = second_pass(OWN)
    own_grad[0] = dk
    own_grad[1] = dv

    keys_t = [jnp.transpose(keys[j]) for j in range(REACH + 1)]
    values_t = [jnp.transpose(values[j]) for j in range(REACH + 1)]
    for h in range(heads):
        columns = pl.ds(h * rows, rows)
        att = sum(dot(values_t[j], weights[j, :, columns]) for j in range(REACH + 1))
        att_ref[:, pl.ds(h * dim, dim)] = jnp.transpose(att).astype(BF16)
        dq = sum(dot(keys_t[j], dscores[j, :, columns]) for j in range(REACH + 1)) * scale
        dq_ref[:, pl.ds(h * dim, dim)] = jnp.transpose(dq).astype(BF16)

    for d in reach:

        @pl.when(me + d < n)
        def _():
            for move in kv_moves(d):
                move.wait_send()
            grad_move(d).wait_recv()
            for which in range(2):
                own_grad[which] += in_grad[d - 1, which].astype(F32)

        @pl.when(me >= d)
        def _():
            grad_move(d).wait_send()

    dk_ref[...] = own_grad[0].astype(BF16)
    dv_ref[...] = own_grad[1].astype(BF16)


def hand_over(*refs):
    count = (len(refs) - 1) // 2
    sem = refs[-1]
    copies = [
        pltpu.make_async_copy(refs[i], refs[count + i], sem.at[i]) for i in range(count)
    ]
    for copy in copies:
        copy.start()
    for copy in copies:
        copy.wait()


def body(n, queries, key_vectors, value_vectors, doc_ids, grad_out):
    rows, width = queries.shape
    dim = key_vectors.shape[1]
    heads = width // dim
    lanes = 128
    doc = doc_ids.reshape(n, rows // lanes, lanes)
    hbm = pl.BlockSpec(memory_space=pltpu.HBM)
    vmem = pl.BlockSpec(memory_space=pltpu.VMEM)
    shapes = [
        jax.ShapeDtypeStruct((rows, width), BF16),
        jax.ShapeDtypeStruct((rows, width), BF16),
        jax.ShapeDtypeStruct((rows, dim), BF16),
        jax.ShapeDtypeStruct((rows, dim), BF16),
    ]
    blocks = REACH + 1
    results = pl.pallas_call(
        functools.partial(kernel, n),
        out_shape=shapes,
        in_specs=[hbm] * 5,
        out_specs=[vmem] * 4,
        scratch_shapes=[
            pltpu.VMEM((heads, rows, dim), BF16),
            pltpu.VMEM((heads, rows, dim), BF16),
            pltpu.VMEM((blocks, rows, dim), BF16),
            pltpu.VMEM((blocks, rows, dim), BF16),
            pltpu.VMEM((blocks, rows // lanes, lanes), jnp.int32),
            pltpu.VMEM((blocks, rows, rows), F32),
            pltpu.VMEM((3, blocks, heads, rows), F32),
            pltpu.VMEM((blocks + 1, heads, rows), F32),
            pltpu.VMEM((blocks, rows, heads * rows), F32),
            pltpu.VMEM((blocks, rows, heads * rows), F32),
            pltpu.VMEM((blocks, rows, heads * rows), BF16),
            pltpu.VMEM((blocks, rows, heads * rows), BF16),
            pltpu.VMEM((2, rows, dim), F32),
            pltpu.VMEM((REACH, 2, rows, dim), BF16),
            pltpu.VMEM((REACH, 2, rows, dim), BF16),
            pltpu.SemaphoreType.DMA((3, 8)),
            pltpu.SemaphoreType.DMA((2, REACH)),
            pltpu.SemaphoreType.DMA((2, REACH)),
            pltpu.SemaphoreType.DMA((REACH,)),
            pltpu.SemaphoreType.DMA((REACH,)),
        ],
        compiler_params=pltpu.CompilerParams(
            collective_id=0, has_side_effects=True, vmem_limit_bytes=48 << 20
        ),
    )(*(pltpu.with_memory_space_constraint(x, pltpu.HBM) for x in (queries, grad_out, key_vectors, value_vectors, doc)))
    return pl.pallas_call(
        hand_over,
        out_shape=shapes,
        in_specs=[vmem] * 4,
        out_specs=[hbm] * 4,
        scratch_shapes=[pltpu.SemaphoreType.DMA((4,))],
        compiler_params=pltpu.CompilerParams(vmem_limit_bytes=8 << 20),
    )(*results)


def solution(mesh):
    return jax.shard_map(
        functools.partial(body, mesh.shape["ctx"]),
        mesh=mesh,
        in_specs=(P("ctx", "head"), P("ctx", "head"), P("ctx", "head"), P(), P("ctx", "head")),
        out_specs=(P("ctx", "head"), P("ctx", "head"), P("ctx", "head"), P("ctx", "head")),
        check_vma=False,
    )
```

```python
import functools
import math

import jax
import jax.numpy as jnp
from jax import lax
from jax.experimental import pallas as pl
from jax.experimental.pallas import tpu as pltpu
from jax.sharding import PartitionSpec as P

REACH = 3
OWN = REACH
F32 = jnp.float32
BF16 = jnp.bfloat16
MESH = pl.DeviceIdType.MESH
NT = (((1,), (1,)), ((), ()))
NN = (((1,), (0,)), ((), ()))


def dot(a, b, dims=NN):
    return lax.dot_general(a, b, dims, preferred_element_type=F32)


def fill_bias(doc, bias):
    rows = doc.shape[2]
    total = doc.shape[1] * rows
    query_doc = jnp.concatenate([doc[OWN, i : i + 1, :] for i in range(doc.shape[1])], axis=1)
    query_doc = jnp.broadcast_to(query_doc, (rows, total))
    for part in range(doc.shape[1]):
        for slot in range(REACH + 1):
            line = jnp.broadcast_to(doc[slot, part : part + 1, :], (rows, rows))
            allowed = jnp.broadcast_to(jnp.transpose(line)[:, 0:1], (rows, total)) == query_doc
            if slot == OWN:
                key_at = lax.broadcasted_iota(jnp.int32, (rows, total), 0) + part * rows
                query_at = lax.broadcasted_iota(jnp.int32, (rows, total), 1)
                allowed = allowed & (key_at <= query_at)
            bias[slot, pl.ds(part * rows, rows), :] = jnp.where(allowed, 0.0, -1e30)


def kernel(
    n,
    q_hbm,
    g_hbm,
    k_hbm,
    v_hbm,
    doc_hbm,
    att_ref,
    dq_ref,
    dk_ref,
    dv_ref,
    q,
    g,
    keys,
    values,
    doc,
    bias,
    stats,
    factors,
    raw,
    slopes,
    weights,
    dscores,
    own_grad,
    out_grad,
    in_grad,
    local_sem,
    kv_send,
    kv_recv,
    grad_send,
    grad_recv,
):
    heads, rows, dim = q.shape
    scale = 1.0 / math.sqrt(dim)
    exponent = math.log2(math.e) * scale
    me = lax.axis_index("ctx")
    reach = range(1, REACH + 1)

    core = lax.rem(me, 2)
    partner = me + 1 - 2 * core
    apart = 3 - 2 * core
    joint = 1 + 2 * core

    barrier = pltpu.get_barrier_semaphore()

    for d in (1, 3):

        @pl.when(me >= d)
        def _():
            pl.semaphore_signal(barrier, inc=1, device_id={"ctx": me - d}, device_id_type=MESH)

    @pl.when(me < n - 3)
    def _():
        pl.semaphore_wait(barrier, 2)

    @pl.when((me >= n - 3) & (me < n - 1))
    def _():
        pl.semaphore_wait(barrier, 1)

    def kv_moves(d, source=None, to=None):
        pairs = ((k_hbm, keys), (v_hbm, values))
        return [
            pltpu.make_async_remote_copy(
                src_ref=given if source is None else held.at[source],
                dst_ref=held.at[REACH - d],
                send_sem=kv_send.at[which, d - 1],
                recv_sem=kv_recv.at[which, d - 1],
                device_id={"ctx": me + d if to is None else to},
                device_id_type=MESH,
            )
            for which, (given, held) in enumerate(pairs)
        ]

    def grad_move(d, to):
        return pltpu.make_async_remote_copy(
            src_ref=out_grad.at[d - 1],
            dst_ref=in_grad.at[d - 1],
            send_sem=grad_send.at[d - 1],
            recv_sem=grad_recv.at[d - 1],
            device_id={"ctx": to},
            device_id_type=MESH,
        )

    @pl.when((core == 0) & (me + 3 < n))
    def _():
        for move in kv_moves(3):
            move.start()

    @pl.when(me + 1 < n)
    def _():
        for move in kv_moves(1):
            move.start()

    local = []
    for slot in range(REACH + 1):
        block = lax.rem(me + n - REACH + slot, n)
        local.append(pltpu.make_async_copy(doc_hbm.at[block], doc.at[slot], local_sem.at[0, slot]))
    local.append(pltpu.make_async_copy(k_hbm, keys.at[OWN], local_sem.at[0, 4]))
    local.append(pltpu.make_async_copy(v_hbm, values.at[OWN], local_sem.at[0, 5]))
    for h in range(heads):
        columns = pl.ds(h * dim, dim)
        local.append(pltpu.make_async_copy(q_hbm.at[:, columns], q.at[h], local_sem.at[1, h]))
        local.append(pltpu.make_async_copy(g_hbm.at[:, columns], g.at[h], local_sem.at[2, h]))
    for copy in local:
        copy.start()

    for d in reach:

        @pl.when(me < d)
        def _():
            keys[REACH - d] = jnp.zeros(keys.shape[1:], BF16)
            values[REACH - d] = jnp.zeros(values.shape[1:], BF16)

    stats[0] = jnp.full(stats.shape[1:], -1e30, F32)
    stats[1] = jnp.zeros(stats.shape[1:], F32)
    stats[2] = jnp.zeros(stats.shape[1:], F32)
    for copy in local[: REACH + 1]:
        copy.wait()
    fill_bias(doc, bias)
    for copy in local[REACH + 1 :]:
        copy.wait()

    def first_pass(j):
        for h in range(heads):
            columns = pl.ds(h * rows, rows)
            s = dot(keys[j], q[h], NT) + bias[j]
            top = s.max(axis=0, keepdims=True)
            e = jnp.exp2((s - top) * exponent)
            slope = dot(values[j], g[h], NT)
            stats[0, j, h : h + 1, :] = top
            stats[1, j, h : h + 1, :] = e.sum(axis=0, keepdims=True)
            stats[2, j, h : h + 1, :] = (e * slope).sum(axis=0, keepdims=True)
            raw[j, :, columns] = e
            slopes[j, :, columns] = slope

    first_pass(OWN)

    @pl.when((core == 1) & (me + 3 < n))
    def _():
        for move in kv_moves(1):
            move.wait_send()
        for move in kv_moves(3):
            move.start()

    @pl.when(core == 1)
    def _():
        for move in kv_moves(1):
            move.wait_recv()
        first_pass(REACH - 1)

    @pl.when(me >= joint)
    def _():
        taken = kv_moves(joint)
        given = kv_moves(2, REACH - joint, partner)
        for arrived, passed in zip(taken, given):
            arrived.wait_recv()
            passed.start()
        first_pass(REACH - joint)

    @pl.when(me >= 2)
    def _():
        for move in kv_moves(2):
            move.wait_recv()
        first_pass(REACH - 2)

    @pl.when((core == 0) & (me >= 3))
    def _():
        for move in kv_moves(3):
            move.wait_recv()
        first_pass(REACH - 3)

    tops = [stats[0, j] for j in range(REACH + 1)]
    top = jnp.maximum(jnp.maximum(tops[0], tops[1]), jnp.maximum(tops[2], tops[3]))
    grown = [jnp.exp2((x - top) * exponent) for x in tops]
    inverse = 1.0 / sum(x * stats[1, j] for j, x in enumerate(grown))
    delta = sum(x * stats[2, j] for j, x in enumerate(grown)) * inverse
    for j in range(REACH + 1):
        factors[j] = grown[j] * inverse
    factors[REACH + 1] = delta

    def second_pass(j):
        for h in range(heads):
            columns = pl.ds(h * rows, rows)
            w = raw[j, :, columns] * factors[j, h : h + 1, :]
            weights[j, :, columns] = w.astype(BF16)
            ds = w * (slopes[j, :, columns] - factors[REACH + 1, h : h + 1, :])
            dscores[j, :, columns] = ds.astype(BF16)
        dv = dot(weights[j], g[...].reshape(heads * rows, dim))
        dk = dot(dscores[j], q[...].reshape(heads * rows, dim)) * scale
        return dk, dv

    for d in reach:

        @pl.when(me < d)
        def _():
            weights[REACH - d] = jnp.zeros(weights.shape[1:], BF16)
            dscores[REACH - d] = jnp.zeros(dscores.shape[1:], BF16)

    @pl.when(me >= 2)
    def _():
        dk, dv = second_pass(REACH - 2)
        out_grad[1, 0] = dk.astype(BF16)
        out_grad[1, 1] = dv.astype(BF16)
        grad_move(2, partner).start()

    @pl.when(me >= apart)
    def _():
        dk, dv = second_pass(REACH - apart)
        out_grad[apart - 1, 0] = dk.astype(BF16)
        out_grad[apart - 1, 1] = dv.astype(BF16)
        grad_move(apart, me - apart).start()

    @pl.when(me >= joint)
    def _():
        dk, dv = second_pass(REACH - joint)
        grad_move(2, partner).wait_recv()
        out_grad[joint - 1, 0] = (dk + in_grad[1, 0].astype(F32)).astype(BF16)
        out_grad[joint - 1, 1] = (dv + in_grad[1, 1].astype(F32)).astype(BF16)
        grad_move(joint, me - joint).start()

    dk, dv = second_pass(OWN)
    own_grad[0] = dk
    own_grad[1] = dv

    keys_t = [jnp.transpose(keys[j]) for j in range(REACH + 1)]
    values_t = [jnp.transpose(values[j]) for j in range(REACH + 1)]
    for h in range(heads):
        columns = pl.ds(h * rows, rows)
        att = sum(dot(values_t[j], weights[j, :, columns]) for j in range(REACH + 1))
        att_ref[:, pl.ds(h * dim, dim)] = jnp.transpose(att).astype(BF16)
        dq = sum(dot(keys_t[j], dscores[j, :, columns]) for j in range(REACH + 1)) * scale
        dq_ref[:, pl.ds(h * dim, dim)] = jnp.transpose(dq).astype(BF16)

    @pl.when((me + 1 < n) & ((core == 0) | (me + 3 >= n)))
    def _():
        for move in kv_moves(1):
            move.wait_send()

    @pl.when(me + 3 < n)
    def _():
        for move in kv_moves(3):
            move.wait_send()

    @pl.when(me >= joint)
    def _():
        for move in kv_moves(2, REACH - joint, partner):
            move.wait_send()
        grad_move(2, partner).wait_send()
        grad_move(joint, me - joint).wait_send()

    @pl.when(me >= apart)
    def _():
        grad_move(apart, me - apart).wait_send()

    for d in (1, 3):

        @pl.when(me + d < n)
        def _():
            grad_move(d, me).wait_recv()
            for which in range(2):
                own_grad[which] += in_grad[d - 1, which].astype(F32)

    dk_ref[...] = own_grad[0].astype(BF16)
    dv_ref[...] = own_grad[1].astype(BF16)


def hand_over(*refs):
    count = (len(refs) - 1) // 2
    sem = refs[-1]
    copies = [
        pltpu.make_async_copy(refs[i], refs[count + i], sem.at[i]) for i in range(count)
    ]
    for copy in copies:
        copy.start()
    for copy in copies:
        copy.wait()


def body(n, queries, key_vectors, value_vectors, doc_ids, grad_out):
    rows, width = queries.shape
    dim = key_vectors.shape[1]
    heads = width // dim
    lanes = 128
    doc = doc_ids.reshape(n, rows // lanes, lanes)
    hbm = pl.BlockSpec(memory_space=pltpu.HBM)
    vmem = pl.BlockSpec(memory_space=pltpu.VMEM)
    shapes = [
        jax.ShapeDtypeStruct((rows, width), BF16),
        jax.ShapeDtypeStruct((rows, width), BF16),
        jax.ShapeDtypeStruct((rows, dim), BF16),
        jax.ShapeDtypeStruct((rows, dim), BF16),
    ]
    blocks = REACH + 1
    results = pl.pallas_call(
        functools.partial(kernel, n),
        out_shape=shapes,
        in_specs=[hbm] * 5,
        out_specs=[vmem] * 4,
        scratch_shapes=[
            pltpu.VMEM((heads, rows, dim), BF16),
            pltpu.VMEM((heads, rows, dim), BF16),
            pltpu.VMEM((blocks, rows, dim), BF16),
            pltpu.VMEM((blocks, rows, dim), BF16),
            pltpu.VMEM((blocks, rows // lanes, lanes), jnp.int32),
            pltpu.VMEM((blocks, rows, rows), F32),
            pltpu.VMEM((3, blocks, heads, rows), F32),
            pltpu.VMEM((blocks + 1, heads, rows), F32),
            pltpu.VMEM((blocks, rows, heads * rows), F32),
            pltpu.VMEM((blocks, rows, heads * rows), F32),
            pltpu.VMEM((blocks, rows, heads * rows), BF16),
            pltpu.VMEM((blocks, rows, heads * rows), BF16),
            pltpu.VMEM((2, rows, dim), F32),
            pltpu.VMEM((REACH, 2, rows, dim), BF16),
            pltpu.VMEM((REACH, 2, rows, dim), BF16),
            pltpu.SemaphoreType.DMA((3, 8)),
            pltpu.SemaphoreType.DMA((2, REACH)),
            pltpu.SemaphoreType.DMA((2, REACH)),
            pltpu.SemaphoreType.DMA((REACH,)),
            pltpu.SemaphoreType.DMA((REACH,)),
        ],
        compiler_params=pltpu.CompilerParams(
            collective_id=0, has_side_effects=True, vmem_limit_bytes=48 << 20
        ),
    )(*(pltpu.with_memory_space_constraint(x, pltpu.HBM) for x in (queries, grad_out, key_vectors, value_vectors, doc)))
    return pl.pallas_call(
        hand_over,
        out_shape=shapes,
        in_specs=[vmem] * 4,
        out_specs=[hbm] * 4,
        scratch_shapes=[pltpu.SemaphoreType.DMA((4,))],
        compiler_params=pltpu.CompilerParams(vmem_limit_bytes=8 << 20),
    )(*results)


def solution(mesh):
    return jax.shard_map(
        functools.partial(body, mesh.shape["ctx"]),
        mesh=mesh,
        in_specs=(P("ctx", "head"), P("ctx", "head"), P("ctx", "head"), P(), P("ctx", "head")),
        out_specs=(P("ctx", "head"), P("ctx", "head"), P("ctx", "head"), P("ctx", "head")),
        check_vma=False,
    )
```

```python
import functools
import math

import jax
import jax.numpy as jnp
from jax import lax
from jax.experimental import pallas as pl
from jax.experimental.pallas import tpu as pltpu
from jax.sharding import PartitionSpec as P

REACH = 3
OWN = REACH
F32 = jnp.float32
BF16 = jnp.bfloat16
MESH = pl.DeviceIdType.MESH
NT = (((1,), (1,)), ((), ()))
NN = (((1,), (0,)), ((), ()))


def dot(a, b, dims=NN):
    return lax.dot_general(a, b, dims, preferred_element_type=F32)


def fill_bias(doc, bias):
    rows = doc.shape[2]
    total = doc.shape[1] * rows
    query_doc = jnp.concatenate([doc[OWN, i : i + 1, :] for i in range(doc.shape[1])], axis=1)
    query_doc = jnp.broadcast_to(query_doc, (rows, total))
    for part in range(doc.shape[1]):
        for slot in range(REACH + 1):
            line = jnp.broadcast_to(doc[slot, part : part + 1, :], (rows, rows))
            allowed = jnp.broadcast_to(jnp.transpose(line)[:, 0:1], (rows, total)) == query_doc
            if slot == OWN:
                key_at = lax.broadcasted_iota(jnp.int32, (rows, total), 0) + part * rows
                query_at = lax.broadcasted_iota(jnp.int32, (rows, total), 1)
                allowed = allowed & (key_at <= query_at)
            bias[slot, pl.ds(part * rows, rows), :] = jnp.where(allowed, 0.0, -1e30)


def kernel(
    n,
    q_hbm,
    g_hbm,
    k_hbm,
    v_hbm,
    doc_hbm,
    att_ref,
    dq_ref,
    dk_ref,
    dv_ref,
    q,
    g,
    keys,
    values,
    doc,
    bias,
    stats,
    factors,
    raw,
    slopes,
    weights,
    dscores,
    own_grad,
    pending,
    out_grad,
    in_grad,
    local_sem,
    kv_send,
    kv_recv,
    grad_send,
    grad_recv,
):
    heads, rows, dim = q.shape
    scale = 1.0 / math.sqrt(dim)
    exponent = math.log2(math.e) * scale
    me = lax.axis_index("ctx")
    reach = range(1, REACH + 1)

    core = lax.rem(me, 2)
    partner = me + 1 - 2 * core
    apart = 3 - 2 * core
    joint = 1 + 2 * core

    barrier = pltpu.get_barrier_semaphore()

    for d in (1, 3):

        @pl.when(me >= d)
        def _():
            pl.semaphore_signal(barrier, inc=1, device_id={"ctx": me - d}, device_id_type=MESH)

    @pl.when(me < n - 3)
    def _():
        pl.semaphore_wait(barrier, 2)

    @pl.when((me >= n - 3) & (me < n - 1))
    def _():
        pl.semaphore_wait(barrier, 1)

    def kv_moves(d, source=None, to=None):
        pairs = ((k_hbm, keys), (v_hbm, values))
        return [
            pltpu.make_async_remote_copy(
                src_ref=given if source is None else held.at[source],
                dst_ref=held.at[REACH - d],
                send_sem=kv_send.at[which, d - 1],
                recv_sem=kv_recv.at[which, d - 1],
                device_id={"ctx": me + d if to is None else to},
                device_id_type=MESH,
            )
            for which, (given, held) in enumerate(pairs)
        ]

    def grad_move(which, d, to):
        return pltpu.make_async_remote_copy(
            src_ref=out_grad.at[d - 1, which],
            dst_ref=in_grad.at[d - 1, which],
            send_sem=grad_send.at[d - 1, which],
            recv_sem=grad_recv.at[d - 1, which],
            device_id={"ctx": to},
            device_id_type=MESH,
        )

    @pl.when((core == 0) & (me + 3 < n))
    def _():
        for move in kv_moves(3):
            move.start()

    @pl.when(me + 1 < n)
    def _():
        for move in kv_moves(1):
            move.start()

    local = []
    for slot in range(REACH + 1):
        block = lax.rem(me + n - REACH + slot, n)
        local.append(pltpu.make_async_copy(doc_hbm.at[block], doc.at[slot], local_sem.at[0, slot]))
    local.append(pltpu.make_async_copy(k_hbm, keys.at[OWN], local_sem.at[0, 4]))
    local.append(pltpu.make_async_copy(v_hbm, values.at[OWN], local_sem.at[0, 5]))
    for h in range(heads):
        columns = pl.ds(h * dim, dim)
        local.append(pltpu.make_async_copy(q_hbm.at[:, columns], q.at[h], local_sem.at[1, h]))
        local.append(pltpu.make_async_copy(g_hbm.at[:, columns], g.at[h], local_sem.at[2, h]))
    for copy in local:
        copy.start()

    for d in reach:

        @pl.when(me < d)
        def _():
            keys[REACH - d] = jnp.zeros(keys.shape[1:], BF16)
            values[REACH - d] = jnp.zeros(values.shape[1:], BF16)

    stats[0] = jnp.full(stats.shape[1:], -1e30, F32)
    stats[1] = jnp.zeros(stats.shape[1:], F32)
    stats[2] = jnp.zeros(stats.shape[1:], F32)
    for copy in local[: REACH + 1]:
        copy.wait()
    fill_bias(doc, bias)
    for copy in local[REACH + 1 :]:
        copy.wait()

    def first_pass(j, keys_here=None, values_here=None):
        if keys_here is not None:
            keys_here()
        for h in range(heads):
            columns = pl.ds(h * rows, rows)
            s = dot(keys[j], q[h], NT) + bias[j]
            top = s.max(axis=0, keepdims=True)
            e = jnp.exp2((s - top) * exponent)
            stats[0, j, h : h + 1, :] = top
            stats[1, j, h : h + 1, :] = e.sum(axis=0, keepdims=True)
            raw[j, :, columns] = e
        if values_here is not None:
            values_here()
        for h in range(heads):
            columns = pl.ds(h * rows, rows)
            slope = dot(values[j], g[h], NT)
            stats[2, j, h : h + 1, :] = (raw[j, :, columns] * slope).sum(axis=0, keepdims=True)
            slopes[j, :, columns] = slope

    first_pass(OWN)

    @pl.when((core == 1) & (me + 3 < n))
    def _():
        for move in kv_moves(1):
            move.wait_send()
        for move in kv_moves(3):
            move.start()

    @pl.when(core == 1)
    def _():
        first_pass(REACH - 1, *(move.wait_recv for move in kv_moves(1)))

    @pl.when(me >= joint)
    def _():
        given = kv_moves(2, REACH - joint, partner)

        def arrive(which, move):
            move.wait_recv()
            given[which].start()

        steps = [functools.partial(arrive, i, move) for i, move in enumerate(kv_moves(joint))]
        first_pass(REACH - joint, *steps)

    @pl.when(me >= 2)
    def _():
        first_pass(REACH - 2, *(move.wait_recv for move in kv_moves(2)))

    @pl.when((core == 0) & (me >= 3))
    def _():
        first_pass(REACH - 3, *(move.wait_recv for move in kv_moves(3)))

    tops = [stats[0, j] for j in range(REACH + 1)]
    top = jnp.maximum(jnp.maximum(tops[0], tops[1]), jnp.maximum(tops[2], tops[3]))
    grown = [jnp.exp2((x - top) * exponent) for x in tops]
    inverse = 1.0 / sum(x * stats[1, j] for j, x in enumerate(grown))
    delta = sum(x * stats[2, j] for j, x in enumerate(grown)) * inverse
    for j in range(REACH + 1):
        factors[j] = grown[j] * inverse
    factors[REACH + 1] = delta

    def second_pass(j, take):
        for h in range(heads):
            columns = pl.ds(h * rows, rows)
            w = raw[j, :, columns] * factors[j, h : h + 1, :]
            weights[j, :, columns] = w.astype(BF16)
        take(1, dot(weights[j], g[...].reshape(heads * rows, dim)))
        for h in range(heads):
            columns = pl.ds(h * rows, rows)
            w = raw[j, :, columns] * factors[j, h : h + 1, :]
            slope = slopes[j, :, columns] - factors[REACH + 1, h : h + 1, :]
            dscores[j, :, columns] = (w * slope).astype(BF16)
        take(0, dot(dscores[j], q[...].reshape(heads * rows, dim)) * scale)

    for d in reach:

        @pl.when(me < d)
        def _():
            weights[REACH - d] = jnp.zeros(weights.shape[1:], BF16)
            dscores[REACH - d] = jnp.zeros(dscores.shape[1:], BF16)

    def alone(d, to):
        def take(which, grad):
            out_grad[d - 1, which] = grad.astype(BF16)
            grad_move(which, d, to).start()

        second_pass(REACH - d, take)

    def hold(which, grad):
        pending[which] = grad

    def join(d):
        for which in (1, 0):
            grad_move(which, 2, partner).wait_recv()
            total = pending[which] + in_grad[1, which].astype(F32)
            out_grad[d - 1, which] = total.astype(BF16)
            grad_move(which, d, me - d).start()

    def keep(which, grad):
        own_grad[which] = grad

    @pl.when((core == 0) & (me >= 2))
    def _():
        second_pass(REACH - 1, hold)
        alone(2, partner)
        join(1)

    @pl.when((core == 0) & (me >= 3))
    def _():
        alone(3, me - 3)

    @pl.when((core == 1) & (me >= 3))
    def _():
        alone(2, partner)
        second_pass(REACH - 3, hold)

    @pl.when(core == 1)
    def _():
        alone(1, me - 1)

    @pl.when((core == 1) & (me >= 3))
    def _():
        join(3)

    second_pass(OWN, keep)

    keys_t = [jnp.transpose(keys[j]) for j in range(REACH + 1)]
    values_t = [jnp.transpose(values[j]) for j in range(REACH + 1)]
    for h in range(heads):
        columns = pl.ds(h * rows, rows)
        att = sum(dot(values_t[j], weights[j, :, columns]) for j in range(REACH + 1))
        att_ref[:, pl.ds(h * dim, dim)] = jnp.transpose(att).astype(BF16)
        dq = sum(dot(keys_t[j], dscores[j, :, columns]) for j in range(REACH + 1)) * scale
        dq_ref[:, pl.ds(h * dim, dim)] = jnp.transpose(dq).astype(BF16)

    @pl.when((me + 1 < n) & ((core == 0) | (me + 3 >= n)))
    def _():
        for move in kv_moves(1):
            move.wait_send()

    @pl.when(me + 3 < n)
    def _():
        for move in kv_moves(3):
            move.wait_send()

    @pl.when(me >= joint)
    def _():
        for move in kv_moves(2, REACH - joint, partner):
            move.wait_send()
        for which in range(2):
            grad_move(which, 2, partner).wait_send()
            grad_move(which, joint, me - joint).wait_send()

    @pl.when(me >= apart)
    def _():
        for which in range(2):
            grad_move(which, apart, me - apart).wait_send()

    for d in (3, 1):

        @pl.when(me + d < n)
        def _():
            for which in (1, 0):
                grad_move(which, d, me).wait_recv()
                own_grad[which] += in_grad[d - 1, which].astype(F32)

    dk_ref[...] = own_grad[0].astype(BF16)
    dv_ref[...] = own_grad[1].astype(BF16)


def hand_over(*refs):
    count = (len(refs) - 1) // 2
    sem = refs[-1]
    copies = [
        pltpu.make_async_copy(refs[i], refs[count + i], sem.at[i]) for i in range(count)
    ]
    for copy in copies:
        copy.start()
    for copy in copies:
        copy.wait()


def body(n, queries, key_vectors, value_vectors, doc_ids, grad_out):
    rows, width = queries.shape
    dim = key_vectors.shape[1]
    heads = width // dim
    lanes = 128
    doc = doc_ids.reshape(n, rows // lanes, lanes)
    hbm = pl.BlockSpec(memory_space=pltpu.HBM)
    vmem = pl.BlockSpec(memory_space=pltpu.VMEM)
    shapes = [
        jax.ShapeDtypeStruct((rows, width), BF16),
        jax.ShapeDtypeStruct((rows, width), BF16),
        jax.ShapeDtypeStruct((rows, dim), BF16),
        jax.ShapeDtypeStruct((rows, dim), BF16),
    ]
    blocks = REACH + 1
    results = pl.pallas_call(
        functools.partial(kernel, n),
        out_shape=shapes,
        in_specs=[hbm] * 5,
        out_specs=[vmem] * 4,
        scratch_shapes=[
            pltpu.VMEM((heads, rows, dim), BF16),
            pltpu.VMEM((heads, rows, dim), BF16),
            pltpu.VMEM((blocks, rows, dim), BF16),
            pltpu.VMEM((blocks, rows, dim), BF16),
            pltpu.VMEM((blocks, rows // lanes, lanes), jnp.int32),
            pltpu.VMEM((blocks, rows, rows), F32),
            pltpu.VMEM((3, blocks, heads, rows), F32),
            pltpu.VMEM((blocks + 1, heads, rows), F32),
            pltpu.VMEM((blocks, rows, heads * rows), F32),
            pltpu.VMEM((blocks, rows, heads * rows), F32),
            pltpu.VMEM((blocks, rows, heads * rows), BF16),
            pltpu.VMEM((blocks, rows, heads * rows), BF16),
            pltpu.VMEM((2, rows, dim), F32),
            pltpu.VMEM((2, rows, dim), F32),
            pltpu.VMEM((REACH, 2, rows, dim), BF16),
            pltpu.VMEM((REACH, 2, rows, dim), BF16),
            pltpu.SemaphoreType.DMA((3, 8)),
            pltpu.SemaphoreType.DMA((2, REACH)),
            pltpu.SemaphoreType.DMA((2, REACH)),
            pltpu.SemaphoreType.DMA((REACH, 2)),
            pltpu.SemaphoreType.DMA((REACH, 2)),
        ],
        compiler_params=pltpu.CompilerParams(
            collective_id=0, has_side_effects=True, vmem_limit_bytes=48 << 20
        ),
    )(*(pltpu.with_memory_space_constraint(x, pltpu.HBM) for x in (queries, grad_out, key_vectors, value_vectors, doc)))
    return pl.pallas_call(
        hand_over,
        out_shape=shapes,
        in_specs=[vmem] * 4,
        out_specs=[hbm] * 4,
        scratch_shapes=[pltpu.SemaphoreType.DMA((4,))],
        compiler_params=pltpu.CompilerParams(vmem_limit_bytes=8 << 20),
    )(*results)


def solution(mesh):
    return jax.shard_map(
        functools.partial(body, mesh.shape["ctx"]),
        mesh=mesh,
        in_specs=(P("ctx", "head"), P("ctx", "head"), P("ctx", "head"), P(), P("ctx", "head")),
        out_specs=(P("ctx", "head"), P("ctx", "head"), P("ctx", "head"), P("ctx", "head")),
        check_vma=False,
    )
```

```python
import functools
import math

import jax
import jax.numpy as jnp
from jax import lax
from jax.experimental import pallas as pl
from jax.experimental.pallas import tpu as pltpu
from jax.sharding import PartitionSpec as P

REACH = 3
OWN = REACH
F32 = jnp.float32
BF16 = jnp.bfloat16
MESH = pl.DeviceIdType.MESH
NT = (((1,), (1,)), ((), ()))
NN = (((1,), (0,)), ((), ()))


def dot(a, b, dims=NN):
    return lax.dot_general(a, b, dims, preferred_element_type=F32)


def fill_bias(doc, bias):
    rows = doc.shape[2]
    total = doc.shape[1] * rows
    query_doc = jnp.concatenate([doc[OWN, i : i + 1, :] for i in range(doc.shape[1])], axis=1)
    query_doc = jnp.broadcast_to(query_doc, (rows, total))
    for part in range(doc.shape[1]):
        for slot in range(REACH + 1):
            line = jnp.broadcast_to(doc[slot, part : part + 1, :], (rows, rows))
            allowed = jnp.broadcast_to(jnp.transpose(line)[:, 0:1], (rows, total)) == query_doc
            if slot == OWN:
                key_at = lax.broadcasted_iota(jnp.int32, (rows, total), 0) + part * rows
                query_at = lax.broadcasted_iota(jnp.int32, (rows, total), 1)
                allowed = allowed & (key_at <= query_at)
            bias[slot, pl.ds(part * rows, rows), :] = jnp.where(allowed, 0.0, -1e30)


def kernel(
    n,
    q_hbm,
    g_hbm,
    k_hbm,
    v_hbm,
    doc_hbm,
    att_ref,
    dq_ref,
    dk_ref,
    dv_ref,
    q,
    g,
    keys,
    values,
    doc,
    bias,
    stats,
    factors,
    raw,
    slopes,
    weights,
    dscores,
    own_grad,
    pending,
    out_grad,
    in_grad,
    local_sem,
    kv_send,
    kv_recv,
    grad_send,
    grad_recv,
):
    heads, rows, dim = q.shape
    scale = 1.0 / math.sqrt(dim)
    exponent = math.log2(math.e) * scale
    me = lax.axis_index("ctx")
    reach = range(1, REACH + 1)

    core = lax.rem(me, 2)
    partner = me + 1 - 2 * core
    apart = 3 - 2 * core
    joint = 1 + 2 * core

    barrier = pltpu.get_barrier_semaphore()

    for d in (1, 3):

        @pl.when(me >= d)
        def _():
            pl.semaphore_signal(barrier, inc=1, device_id={"ctx": me - d}, device_id_type=MESH)

    @pl.when(me < n - 3)
    def _():
        pl.semaphore_wait(barrier, 2)

    @pl.when((me >= n - 3) & (me < n - 1))
    def _():
        pl.semaphore_wait(barrier, 1)

    def kv_moves(d, source=None, to=None):
        pairs = ((k_hbm, keys), (v_hbm, values))
        return [
            pltpu.make_async_remote_copy(
                src_ref=given if source is None else held.at[source],
                dst_ref=held.at[REACH - d],
                send_sem=kv_send.at[which, d - 1],
                recv_sem=kv_recv.at[which, d - 1],
                device_id={"ctx": me + d if to is None else to},
                device_id_type=MESH,
            )
            for which, (given, held) in enumerate(pairs)
        ]

    def grad_move(which, d, to):
        return pltpu.make_async_remote_copy(
            src_ref=out_grad.at[d - 1, which],
            dst_ref=in_grad.at[d - 1, which],
            send_sem=grad_send.at[d - 1, which],
            recv_sem=grad_recv.at[d - 1, which],
            device_id={"ctx": to},
            device_id_type=MESH,
        )

    @pl.when((core == 0) & (me + 3 < n))
    def _():
        for move in kv_moves(3):
            move.start()

    @pl.when(me + 1 < n)
    def _():
        for move in kv_moves(1):
            move.start()

    local = []
    for slot in range(REACH + 1):
        block = lax.rem(me + n - REACH + slot, n)
        local.append(pltpu.make_async_copy(doc_hbm.at[block], doc.at[slot], local_sem.at[0, slot]))
    local.append(pltpu.make_async_copy(k_hbm, keys.at[OWN], local_sem.at[0, 4]))
    local.append(pltpu.make_async_copy(v_hbm, values.at[OWN], local_sem.at[0, 5]))
    for h in range(heads):
        columns = pl.ds(h * dim, dim)
        local.append(pltpu.make_async_copy(q_hbm.at[:, columns], q.at[h], local_sem.at[1, h]))
        local.append(pltpu.make_async_copy(g_hbm.at[:, columns], g.at[h], local_sem.at[2, h]))
    for copy in local:
        copy.start()

    for d in reach:

        @pl.when(me < d)
        def _():
            keys[REACH - d] = jnp.zeros(keys.shape[1:], BF16)
            values[REACH - d] = jnp.zeros(values.shape[1:], BF16)

    stats[0] = jnp.full(stats.shape[1:], -1e30, F32)
    stats[1] = jnp.zeros(stats.shape[1:], F32)
    stats[2] = jnp.zeros(stats.shape[1:], F32)
    for copy in local[: REACH + 1]:
        copy.wait()
    fill_bias(doc, bias)
    for copy in local[REACH + 1 :]:
        copy.wait()

    def first_pass(j, keys_here=None, values_here=None):
        if keys_here is not None:
            keys_here()
        for h in range(heads):
            columns = pl.ds(h * rows, rows)
            s = dot(keys[j], q[h], NT) + bias[j]
            top = s.max(axis=0, keepdims=True)
            e = jnp.exp2((s - top) * exponent)
            stats[0, j, h : h + 1, :] = top
            stats[1, j, h : h + 1, :] = e.sum(axis=0, keepdims=True)
            raw[j, :, columns] = e
        if values_here is not None:
            values_here()
        for h in range(heads):
            columns = pl.ds(h * rows, rows)
            slope = dot(values[j], g[h], NT)
            stats[2, j, h : h + 1, :] = (raw[j, :, columns] * slope).sum(axis=0, keepdims=True)
            slopes[j, :, columns] = slope

    first_pass(OWN)

    @pl.when((core == 1) & (me + 3 < n))
    def _():
        for move in kv_moves(1):
            move.wait_send()
        for move in kv_moves(3):
            move.start()

    @pl.when(core == 1)
    def _():
        first_pass(REACH - 1, *(move.wait_recv for move in kv_moves(1)))

    early = core * (4 // (me + 1))
    first = joint + early * (2 - joint)
    for d in (first, joint + 2 - first):

        @pl.when(me >= 2)
        def _():
            given = kv_moves(2, REACH - joint, partner)

            def arrive(which, move):
                move.wait_recv()

                @pl.when(d == joint)
                def _():
                    given[which].start()

            steps = [functools.partial(arrive, i, move) for i, move in enumerate(kv_moves(d))]
            first_pass(REACH - d, *steps)

    @pl.when((core == 0) & (me >= 3))
    def _():
        first_pass(REACH - 3, *(move.wait_recv for move in kv_moves(3)))

    tops = [stats[0, j] for j in range(REACH + 1)]
    top = jnp.maximum(jnp.maximum(tops[0], tops[1]), jnp.maximum(tops[2], tops[3]))
    grown = [jnp.exp2((x - top) * exponent) for x in tops]
    inverse = 1.0 / sum(x * stats[1, j] for j, x in enumerate(grown))
    delta = sum(x * stats[2, j] for j, x in enumerate(grown)) * inverse
    for j in range(REACH + 1):
        factors[j] = grown[j] * inverse
    factors[REACH + 1] = delta

    def second_pass(j, take):
        for h in range(heads):
            columns = pl.ds(h * rows, rows)
            w = raw[j, :, columns] * factors[j, h : h + 1, :]
            weights[j, :, columns] = w.astype(BF16)
        take(1, dot(weights[j], g[...].reshape(heads * rows, dim)))
        for h in range(heads):
            columns = pl.ds(h * rows, rows)
            w = raw[j, :, columns] * factors[j, h : h + 1, :]
            slope = slopes[j, :, columns] - factors[REACH + 1, h : h + 1, :]
            dscores[j, :, columns] = (w * slope).astype(BF16)
        take(0, dot(dscores[j], q[...].reshape(heads * rows, dim)) * scale)

    for d in reach:

        @pl.when(me < d)
        def _():
            weights[REACH - d] = jnp.zeros(weights.shape[1:], BF16)
            dscores[REACH - d] = jnp.zeros(dscores.shape[1:], BF16)

    def alone(d, to):
        def take(which, grad):
            out_grad[d - 1, which] = grad.astype(BF16)
            grad_move(which, d, to).start()

        second_pass(REACH - d, take)

    def hold(which, grad):
        pending[which] = grad

    def join(d):
        for which in (1, 0):
            grad_move(which, 2, partner).wait_recv()
            total = pending[which] + in_grad[1, which].astype(F32)
            out_grad[d - 1, which] = total.astype(BF16)
            grad_move(which, d, me - d).start()

    def keep(which, grad):
        own_grad[which] = grad

    @pl.when((core == 0) & (me >= 2))
    def _():
        second_pass(REACH - 1, hold)

    @pl.when(me == 2)
    def _():
        join(1)

    @pl.when((core == 0) & (me >= 2))
    def _():
        alone(2, partner)

    @pl.when((core == 0) & (me > 2))
    def _():
        join(1)

    @pl.when((core == 0) & (me >= 3))
    def _():
        alone(3, me - 3)

    @pl.when((core == 1) & (me >= 3))
    def _():
        alone(2, partner)
        second_pass(REACH - 3, hold)

    @pl.when(core == 1)
    def _():
        alone(1, me - 1)

    @pl.when((core == 1) & (me >= 3))
    def _():
        join(3)

    second_pass(OWN, keep)

    keys_t = [jnp.transpose(keys[j]) for j in range(REACH + 1)]
    values_t = [jnp.transpose(values[j]) for j in range(REACH + 1)]
    for h in range(heads):
        columns = pl.ds(h * rows, rows)
        att = sum(dot(values_t[j], weights[j, :, columns]) for j in range(REACH + 1))
        att_ref[:, pl.ds(h * dim, dim)] = jnp.transpose(att).astype(BF16)
        dq = sum(dot(keys_t[j], dscores[j, :, columns]) for j in range(REACH + 1)) * scale
        dq_ref[:, pl.ds(h * dim, dim)] = jnp.transpose(dq).astype(BF16)

    @pl.when((me + 1 < n) & ((core == 0) | (me + 3 >= n)))
    def _():
        for move in kv_moves(1):
            move.wait_send()

    @pl.when(me + 3 < n)
    def _():
        for move in kv_moves(3):
            move.wait_send()

    @pl.when(me >= joint)
    def _():
        for move in kv_moves(2, REACH - joint, partner):
            move.wait_send()
        for which in range(2):
            grad_move(which, 2, partner).wait_send()
            grad_move(which, joint, me - joint).wait_send()

    @pl.when(me >= apart)
    def _():
        for which in range(2):
            grad_move(which, apart, me - apart).wait_send()

    for d in (3, 1):

        @pl.when(me + d < n)
        def _():
            for which in (1, 0):
                grad_move(which, d, me).wait_recv()
                own_grad[which] += in_grad[d - 1, which].astype(F32)

    dk_ref[...] = own_grad[0].astype(BF16)
    dv_ref[...] = own_grad[1].astype(BF16)


def hand_over(*refs):
    count = (len(refs) - 1) // 2
    sem = refs[-1]
    copies = [
        pltpu.make_async_copy(refs[i], refs[count + i], sem.at[i]) for i in range(count)
    ]
    for copy in copies:
        copy.start()
    for copy in copies:
        copy.wait()


def body(n, queries, key_vectors, value_vectors, doc_ids, grad_out):
    rows, width = queries.shape
    dim = key_vectors.shape[1]
    heads = width // dim
    lanes = 128
    doc = doc_ids.reshape(n, rows // lanes, lanes)
    hbm = pl.BlockSpec(memory_space=pltpu.HBM)
    vmem = pl.BlockSpec(memory_space=pltpu.VMEM)
    shapes = [
        jax.ShapeDtypeStruct((rows, width), BF16),
        jax.ShapeDtypeStruct((rows, width), BF16),
        jax.ShapeDtypeStruct((rows, dim), BF16),
        jax.ShapeDtypeStruct((rows, dim), BF16),
    ]
    blocks = REACH + 1
    results = pl.pallas_call(
        functools.partial(kernel, n),
        out_shape=shapes,
        in_specs=[hbm] * 5,
        out_specs=[vmem] * 4,
        scratch_shapes=[
            pltpu.VMEM((heads, rows, dim), BF16),
            pltpu.VMEM((heads, rows, dim), BF16),
            pltpu.VMEM((blocks, rows, dim), BF16),
            pltpu.VMEM((blocks, rows, dim), BF16),
            pltpu.VMEM((blocks, rows // lanes, lanes), jnp.int32),
            pltpu.VMEM((blocks, rows, rows), F32),
            pltpu.VMEM((3, blocks, heads, rows), F32),
            pltpu.VMEM((blocks + 1, heads, rows), F32),
            pltpu.VMEM((blocks, rows, heads * rows), F32),
            pltpu.VMEM((blocks, rows, heads * rows), F32),
            pltpu.VMEM((blocks, rows, heads * rows), BF16),
            pltpu.VMEM((blocks, rows, heads * rows), BF16),
            pltpu.VMEM((2, rows, dim), F32),
            pltpu.VMEM((2, rows, dim), F32),
            pltpu.VMEM((REACH, 2, rows, dim), BF16),
            pltpu.VMEM((REACH, 2, rows, dim), BF16),
            pltpu.SemaphoreType.DMA((3, 8)),
            pltpu.SemaphoreType.DMA((2, REACH)),
            pltpu.SemaphoreType.DMA((2, REACH)),
            pltpu.SemaphoreType.DMA((REACH, 2)),
            pltpu.SemaphoreType.DMA((REACH, 2)),
        ],
        compiler_params=pltpu.CompilerParams(
            collective_id=0, has_side_effects=True, vmem_limit_bytes=48 << 20
        ),
    )(*(pltpu.with_memory_space_constraint(x, pltpu.HBM) for x in (queries, grad_out, key_vectors, value_vectors, doc)))
    return pl.pallas_call(
        hand_over,
        out_shape=shapes,
        in_specs=[vmem] * 4,
        out_specs=[hbm] * 4,
        scratch_shapes=[pltpu.SemaphoreType.DMA((4,))],
        compiler_params=pltpu.CompilerParams(vmem_limit_bytes=8 << 20),
    )(*results)


def solution(mesh):
    return jax.shard_map(
        functools.partial(body, mesh.shape["ctx"]),
        mesh=mesh,
        in_specs=(P("ctx", "head"), P("ctx", "head"), P("ctx", "head"), P(), P("ctx", "head")),
        out_specs=(P("ctx", "head"), P("ctx", "head"), P("ctx", "head"), P("ctx", "head")),
        check_vma=False,
    )
```

```python
import functools
import math

import jax
import jax.numpy as jnp
from jax import lax
from jax.experimental import pallas as pl
from jax.experimental.pallas import tpu as pltpu
from jax.sharding import PartitionSpec as P

REACH = 3
OWN = REACH
F32 = jnp.float32
BF16 = jnp.bfloat16
MESH = pl.DeviceIdType.MESH
NT = (((1,), (1,)), ((), ()))
NN = (((1,), (0,)), ((), ()))


def dot(a, b, dims=NN):
    return lax.dot_general(a, b, dims, preferred_element_type=F32)


def fill_bias(doc, bias):
    rows = doc.shape[2]
    total = doc.shape[1] * rows
    query_doc = jnp.concatenate([doc[OWN, i : i + 1, :] for i in range(doc.shape[1])], axis=1)
    query_doc = jnp.broadcast_to(query_doc, (rows, total))
    for part in range(doc.shape[1]):
        for slot in range(REACH + 1):
            line = jnp.broadcast_to(doc[slot, part : part + 1, :], (rows, rows))
            allowed = jnp.broadcast_to(jnp.transpose(line)[:, 0:1], (rows, total)) == query_doc
            if slot == OWN:
                key_at = lax.broadcasted_iota(jnp.int32, (rows, total), 0) + part * rows
                query_at = lax.broadcasted_iota(jnp.int32, (rows, total), 1)
                allowed = allowed & (key_at <= query_at)
            bias[slot, pl.ds(part * rows, rows), :] = jnp.where(allowed, 0.0, -1e30)


def kernel(
    n,
    q_hbm,
    g_hbm,
    k_hbm,
    v_hbm,
    doc_hbm,
    att_ref,
    dq_ref,
    dk_ref,
    dv_ref,
    q,
    g,
    keys,
    values,
    doc,
    bias,
    stats,
    factors,
    raw,
    slopes,
    weights,
    dscores,
    own_grad,
    pending,
    out_grad,
    in_grad,
    local_sem,
    kv_send,
    kv_recv,
    grad_send,
    grad_recv,
):
    heads, rows, dim = q.shape
    scale = 1.0 / math.sqrt(dim)
    exponent = math.log2(math.e) * scale
    me = lax.axis_index("ctx")
    reach = range(1, REACH + 1)

    core = lax.rem(me, 2)
    partner = me + 1 - 2 * core
    apart = 3 - 2 * core
    joint = 1 + 2 * core

    barrier = pltpu.get_barrier_semaphore()

    for d in (1, 3):

        @pl.when(me >= d)
        def _():
            pl.semaphore_signal(barrier, inc=1, device_id={"ctx": me - d}, device_id_type=MESH)

    @pl.when(me < n - 3)
    def _():
        pl.semaphore_wait(barrier, 2)

    @pl.when((me >= n - 3) & (me < n - 1))
    def _():
        pl.semaphore_wait(barrier, 1)

    def kv_moves(d, source=None, to=None):
        pairs = ((k_hbm, keys), (v_hbm, values))
        return [
            pltpu.make_async_remote_copy(
                src_ref=given if source is None else held.at[source],
                dst_ref=held.at[REACH - d],
                send_sem=kv_send.at[which, d - 1],
                recv_sem=kv_recv.at[which, d - 1],
                device_id={"ctx": me + d if to is None else to},
                device_id_type=MESH,
            )
            for which, (given, held) in enumerate(pairs)
        ]

    def grad_move(which, d, to):
        return pltpu.make_async_remote_copy(
            src_ref=out_grad.at[d - 1, which],
            dst_ref=in_grad.at[d - 1, which],
            send_sem=grad_send.at[d - 1, which],
            recv_sem=grad_recv.at[d - 1, which],
            device_id={"ctx": to},
            device_id_type=MESH,
        )

    @pl.when((core == 0) & (me + 3 < n))
    def _():
        for move in kv_moves(3):
            move.start()

    @pl.when(me + 1 < n)
    def _():
        for move in kv_moves(1):
            move.start()

    local = []
    for slot in range(REACH + 1):
        block = lax.rem(me + n - REACH + slot, n)
        local.append(pltpu.make_async_copy(doc_hbm.at[block], doc.at[slot], local_sem.at[0, slot]))
    local.append(pltpu.make_async_copy(k_hbm, keys.at[OWN], local_sem.at[0, 4]))
    local.append(pltpu.make_async_copy(v_hbm, values.at[OWN], local_sem.at[0, 5]))
    for h in range(heads):
        columns = pl.ds(h * dim, dim)
        local.append(pltpu.make_async_copy(q_hbm.at[:, columns], q.at[h], local_sem.at[1, h]))
        local.append(pltpu.make_async_copy(g_hbm.at[:, columns], g.at[h], local_sem.at[2, h]))
    for copy in local:
        copy.start()

    for d in reach:

        @pl.when(me < d)
        def _():
            keys[REACH - d] = jnp.zeros(keys.shape[1:], BF16)
            values[REACH - d] = jnp.zeros(values.shape[1:], BF16)

    stats[0] = jnp.full(stats.shape[1:], -1e30, F32)
    stats[1] = jnp.zeros(stats.shape[1:], F32)
    stats[2] = jnp.zeros(stats.shape[1:], F32)
    for copy in local[: REACH + 1]:
        copy.wait()
    fill_bias(doc, bias)
    for copy in local[REACH + 1 :]:
        copy.wait()

    def key_pass(j):
        for h in range(heads):
            columns = pl.ds(h * rows, rows)
            s = dot(keys[j], q[h], NT) + bias[j]
            top = s.max(axis=0, keepdims=True)
            e = jnp.exp2((s - top) * exponent)
            stats[0, j, h : h + 1, :] = top
            stats[1, j, h : h + 1, :] = e.sum(axis=0, keepdims=True)
            raw[j, :, columns] = e

    def value_pass(j):
        for h in range(heads):
            columns = pl.ds(h * rows, rows)
            slope = dot(values[j], g[h], NT)
            stats[2, j, h : h + 1, :] = (raw[j, :, columns] * slope).sum(axis=0, keepdims=True)
            slopes[j, :, columns] = slope

    def arrive(which, d, passing=False):
        kv_moves(d)[which].wait_recv()
        if passing:

            @pl.when(d == joint)
            def _():
                kv_moves(2, REACH - joint, partner)[which].start()

        (key_pass, value_pass)[which](REACH - d)

    key_pass(OWN)
    value_pass(OWN)

    @pl.when((core == 1) & (me + 3 < n))
    def _():
        for move in kv_moves(1):
            move.wait_send()
        for move in kv_moves(3):
            move.start()

    @pl.when(core == 1)
    def _():
        arrive(0, 1)
        arrive(1, 1)

    early = core * (4 // (me + 1))
    first = joint + early * (2 - joint)
    second = joint + 2 - first

    @pl.when(me >= 2)
    def _():
        arrive(0, first, True)
        arrive(1, first, True)
        arrive(0, second, True)

    @pl.when((core == 0) & (me >= 3))
    def _():
        arrive(0, 3)

    tops = [stats[0, j] for j in range(REACH + 1)]
    top = jnp.maximum(jnp.maximum(tops[0], tops[1]), jnp.maximum(tops[2], tops[3]))
    grown = [jnp.exp2((x - top) * exponent) for x in tops]
    inverse = 1.0 / sum(x * stats[1, j] for j, x in enumerate(grown))
    for j in range(REACH + 1):
        factors[j] = grown[j] * inverse

    def weight_pass(j, take):
        for h in range(heads):
            columns = pl.ds(h * rows, rows)
            w = raw[j, :, columns] * factors[j, h : h + 1, :]
            weights[j, :, columns] = w.astype(BF16)
        take(1, dot(weights[j], g[...].reshape(heads * rows, dim)))

    def score_pass(j, take):
        for h in range(heads):
            columns = pl.ds(h * rows, rows)
            w = raw[j, :, columns] * factors[j, h : h + 1, :]
            slope = slopes[j, :, columns] - factors[REACH + 1, h : h + 1, :]
            dscores[j, :, columns] = (w * slope).astype(BF16)
        take(0, dot(dscores[j], q[...].reshape(heads * rows, dim)) * scale)

    def second_pass(j, take):
        weight_pass(j, take)
        score_pass(j, take)

    for d in reach:

        @pl.when(me < d)
        def _():
            weights[REACH - d] = jnp.zeros(weights.shape[1:], BF16)
            dscores[REACH - d] = jnp.zeros(dscores.shape[1:], BF16)

    def away(d, to):
        def take(which, grad):
            out_grad[d - 1, which] = grad.astype(BF16)
            grad_move(which, d, to).start()

        return take

    def hold(which, grad):
        pending[which] = grad

    def join(d, which):
        grad_move(which, 2, partner).wait_recv()
        total = pending[which] + in_grad[1, which].astype(F32)
        out_grad[d - 1, which] = total.astype(BF16)
        grad_move(which, d, me - d).start()

    def keep(which, grad):
        own_grad[which] = grad

    def lead(step, which):
        @pl.when((core == 0) & (me >= 2))
        def _():
            step(REACH - 1, hold)

        @pl.when(me == 2)
        def _():
            join(1, which)

        @pl.when((core == 1) & (me >= 3))
        def _():
            step(REACH - 2, away(2, partner))

    lead(weight_pass, 1)

    @pl.when(me >= 2)
    def _():
        arrive(1, second, True)

    @pl.when((core == 0) & (me >= 3))
    def _():
        arrive(1, 3)

    factors[REACH + 1] = sum(factors[j] * stats[2, j] for j in range(REACH + 1))
    lead(score_pass, 0)

    @pl.when((core == 0) & (me >= 2))
    def _():
        second_pass(REACH - 2, away(2, partner))

    @pl.when((core == 0) & (me > 2))
    def _():
        join(1, 1)
        join(1, 0)
        second_pass(REACH - 3, away(3, me - 3))

    @pl.when((core == 1) & (me >= 3))
    def _():
        second_pass(REACH - 3, hold)

    @pl.when(core == 1)
    def _():
        second_pass(REACH - 1, away(1, me - 1))

    @pl.when((core == 1) & (me >= 3))
    def _():
        join(3, 1)
        join(3, 0)

    second_pass(OWN, keep)

    keys_t = [jnp.transpose(keys[j]) for j in range(REACH + 1)]
    values_t = [jnp.transpose(values[j]) for j in range(REACH + 1)]
    for h in range(heads):
        columns = pl.ds(h * rows, rows)
        att = sum(dot(values_t[j], weights[j, :, columns]) for j in range(REACH + 1))
        att_ref[:, pl.ds(h * dim, dim)] = jnp.transpose(att).astype(BF16)
        dq = sum(dot(keys_t[j], dscores[j, :, columns]) for j in range(REACH + 1)) * scale
        dq_ref[:, pl.ds(h * dim, dim)] = jnp.transpose(dq).astype(BF16)

    @pl.when((me + 1 < n) & ((core == 0) | (me + 3 >= n)))
    def _():
        for move in kv_moves(1):
            move.wait_send()

    @pl.when(me + 3 < n)
    def _():
        for move in kv_moves(3):
            move.wait_send()

    @pl.when(me >= joint)
    def _():
        for move in kv_moves(2, REACH - joint, partner):
            move.wait_send()
        for which in range(2):
            grad_move(which, 2, partner).wait_send()
            grad_move(which, joint, me - joint).wait_send()

    @pl.when(me >= apart)
    def _():
        for which in range(2):
            grad_move(which, apart, me - apart).wait_send()

    for d in (3, 1):

        @pl.when(me + d < n)
        def _():
            for which in (1, 0):
                grad_move(which, d, me).wait_recv()
                own_grad[which] += in_grad[d - 1, which].astype(F32)

    dk_ref[...] = own_grad[0].astype(BF16)
    dv_ref[...] = own_grad[1].astype(BF16)


def hand_over(*refs):
    count = (len(refs) - 1) // 2
    sem = refs[-1]
    copies = [
        pltpu.make_async_copy(refs[i], refs[count + i], sem.at[i]) for i in range(count)
    ]
    for copy in copies:
        copy.start()
    for copy in copies:
        copy.wait()


def body(n, queries, key_vectors, value_vectors, doc_ids, grad_out):
    rows, width = queries.shape
    dim = key_vectors.shape[1]
    heads = width // dim
    lanes = 128
    doc = doc_ids.reshape(n, rows // lanes, lanes)
    hbm = pl.BlockSpec(memory_space=pltpu.HBM)
    vmem = pl.BlockSpec(memory_space=pltpu.VMEM)
    shapes = [
        jax.ShapeDtypeStruct((rows, width), BF16),
        jax.ShapeDtypeStruct((rows, width), BF16),
        jax.ShapeDtypeStruct((rows, dim), BF16),
        jax.ShapeDtypeStruct((rows, dim), BF16),
    ]
    blocks = REACH + 1
    results = pl.pallas_call(
        functools.partial(kernel, n),
        out_shape=shapes,
        in_specs=[hbm] * 5,
        out_specs=[vmem] * 4,
        scratch_shapes=[
            pltpu.VMEM((heads, rows, dim), BF16),
            pltpu.VMEM((heads, rows, dim), BF16),
            pltpu.VMEM((blocks, rows, dim), BF16),
            pltpu.VMEM((blocks, rows, dim), BF16),
            pltpu.VMEM((blocks, rows // lanes, lanes), jnp.int32),
            pltpu.VMEM((blocks, rows, rows), F32),
            pltpu.VMEM((3, blocks, heads, rows), F32),
            pltpu.VMEM((blocks + 1, heads, rows), F32),
            pltpu.VMEM((blocks, rows, heads * rows), F32),
            pltpu.VMEM((blocks, rows, heads * rows), F32),
            pltpu.VMEM((blocks, rows, heads * rows), BF16),
            pltpu.VMEM((blocks, rows, heads * rows), BF16),
            pltpu.VMEM((2, rows, dim), F32),
            pltpu.VMEM((2, rows, dim), F32),
            pltpu.VMEM((REACH, 2, rows, dim), BF16),
            pltpu.VMEM((REACH, 2, rows, dim), BF16),
            pltpu.SemaphoreType.DMA((3, 8)),
            pltpu.SemaphoreType.DMA((2, REACH)),
            pltpu.SemaphoreType.DMA((2, REACH)),
            pltpu.SemaphoreType.DMA((REACH, 2)),
            pltpu.SemaphoreType.DMA((REACH, 2)),
        ],
        compiler_params=pltpu.CompilerParams(
            collective_id=0, has_side_effects=True, vmem_limit_bytes=48 << 20
        ),
    )(*(pltpu.with_memory_space_constraint(x, pltpu.HBM) for x in (queries, grad_out, key_vectors, value_vectors, doc)))
    return pl.pallas_call(
        hand_over,
        out_shape=shapes,
        in_specs=[vmem] * 4,
        out_specs=[hbm] * 4,
        scratch_shapes=[pltpu.SemaphoreType.DMA((4,))],
        compiler_params=pltpu.CompilerParams(vmem_limit_bytes=8 << 20),
    )(*results)


def solution(mesh):
    return jax.shard_map(
        functools.partial(body, mesh.shape["ctx"]),
        mesh=mesh,
        in_specs=(P("ctx", "head"), P("ctx", "head"), P("ctx", "head"), P(), P("ctx", "head")),
        out_specs=(P("ctx", "head"), P("ctx", "head"), P("ctx", "head"), P("ctx", "head")),
        check_vma=False,
    )
```
